512 devices in a mesh: dp: 16 (over z, core), tp: 4 (over y_lo), cp: 8 (over y_hi, x).
Axes of the slice: x: 4, y: 8 (y_hi: 2, y_lo: 4; y = y_hi * 4 + y_lo), z: 8, core: 2. Of those that a mesh axis runs over, the one named last changes fastest.
Arguments:
- tokens: bfloat16 [65536, 1024], P(('dp', 'tp', 'cp')), may hold values from -6 to 6
- expert_ids: int32 [65536, 2], P(('dp', 'tp', 'cp')), may hold values from 0 to 31, all different within a row; in each aligned block of 128 rows (0 to 127, 128 to 255, ...) at most 12 rows name the same one
- router_weight: bfloat16 [1024, 32], replicated, may hold values from -0.1875 to 0.1875
- gate_weight: bfloat16 [32, 1024, 384], P(('tp', 'cp'), 'dp'), may hold values from -0.1875 to 0.1875
- up_weight: bfloat16 [32, 1024, 384], P(('tp', 'cp'), 'dp'), may hold values from -0.1875 to 0.1875
- down_weight: bfloat16 [32, 384, 1024], P(('tp', 'cp'), None, 'dp'), may hold values from -0.3125 to 0.3125
- grad_out: bfloat16 [65536, 1024], P(('dp', 'tp', 'cp')), may hold values from -6 to 6
Outputs:
- moe_out: bfloat16 [65536, 1024], P(('dp', 'tp', 'cp'))
- grad_tokens: bfloat16 [65536, 1024], P(('dp', 'tp', 'cp'))
- router_grad: float32 [1024, 32], replicated
The draws below stay inside these ranges and needn't reach their ends.
Inputs may be any that keep to these rules, and one draw needn't show every extreme that they name: `expert_ids`: each row names 2 different experts. Among the 128 rows of one device no expert is named by more than 12 rows, a bound that some block reaches.
All inputs are finite; a program needn't handle non-finite values.
Results may differ from the reference program's by a relative error of at most 0.0064.
Values may be sent and summed in bfloat16 or wider, within the bound.
A program may use at most 64 MiB of HBM per device.

```python
import math
import jax
import jax.numpy as jnp
import numpy as np
from jax import lax

D = 1024
FF = 384
TOK_DEV = 128
TOPK = 2
EXPERTS = 32
CAP = 12
TOKENS = 65536


def level_of(key, extent, cuts, least, largest):
    gain, own = 1.0, jax.random.fold_in(key, 6)
    for dim, parts in cuts:
        steps = jnp.exp(jax.random.uniform(jax.random.fold_in(own, dim), (parts,), jnp.float32, least / len(cuts), largest / len(cuts)))
        gain = gain * jnp.repeat(steps, extent[dim] // parts).reshape([-1 if axis == dim else 1 for axis in range(len(extent))])
    return gain


def deal_out(stream_key, own, number, rows, count, top, most, lean):
    ranking = jax.random.permutation(stream_key, count)
    crowded, usual = portions_of(count, rows * top, most, lean, True), portions_of(count, rows * top, most, lean, False)
    places = jnp.arange(count)

    def named(tallies, offset_by):
        used = int((tallies > 0).sum())
        fixed = max(1, used // 4)
        passed = fixed + (places - fixed + offset_by * (used - fixed)) % max(1, count - fixed)
        return jnp.zeros((count,), jnp.int32).at[ranking[jnp.where(places < fixed, places, passed)]].set(jnp.asarray(tallies, jnp.int32))

    tallies = jnp.where(number % 4 == 0, named(crowded, number // 4), named(usual, number - number // 4 - 1))
    mixed = jax.random.permutation(jax.random.fold_in(own, 3), count)
    source_of, receiver = mixed[0:count // 2 * 2:2], mixed[1:count // 2 * 2:2]
    margin = jnp.minimum(tallies[source_of] - 1, most - tallies[receiver]) // 2
    margin = jnp.where((source_of == ranking[0]) | (receiver == ranking[0]) | (tallies[receiver] == 0), 0, jnp.maximum(margin, 0))
    passed = jax.random.randint(jax.random.fold_in(own, 4), (count // 2,), 0, 1 << 20) % (margin + 1)
    tallies = tallies.at[source_of].add(-passed).at[receiver].add(passed)
    items = jnp.searchsorted(jnp.cumsum(tallies), jnp.arange(rows * top), side="right").astype(jnp.int32)
    table = items.reshape(top, rows).T
    table = table[jax.random.permutation(jax.random.fold_in(own, 1), rows)]
    offset_by = jax.random.randint(jax.random.fold_in(own, 2), (rows, 1), 0, top)
    return jnp.take_along_axis(table, (jnp.arange(top)[None, :] + offset_by) % top, axis=1)


def portions_of(number_of, total, limit, skew, full):
    portions = [(1 << 20) // math.isqrt(grade ** skew) + 1 for grade in range(1, number_of + 1)]
    largest = limit if full else min(limit, max(-(-total // number_of), total * portions[0] // sum(portions)))
    least = 1 if total - largest >= number_of - 1 else 0
    holding, rest = [largest] + [least] * (number_of - 1), total - largest - least * (number_of - 1)
    while rest > 0:
        movable = [i for i in range(1, number_of) if holding[i] < largest] or [i for i in range(1, number_of) if holding[i] < limit]
        mass, remaining = sum([portions[i] for i in movable]), rest
        for i in movable:
            more = min(limit - holding[i], max(1, remaining * portions[i] // mass), rest)
            holding[i] = holding[i] + more
            rest = rest - more
    return np.array(holding)


def normal_values(stream_key, dims, scale, most, shards=(), kind=jnp.bfloat16):
    result = scale * jax.random.normal(stream_key, dims, jnp.float32)
    if shards:
        result = result * level_of(stream_key, dims, shards, -0.22, 0.18)
    return jnp.clip(result, -most, most).astype(kind)


def setup_inputs(seed: int = 0) -> dict:
    splits = jax.random.split(jax.random.key(seed), 8)
    tokens = normal_values(splits[0], (TOKENS, D), 1.0, 6.0, ((0, 512),))
    expert_ids_keys = jax.random.split(jax.random.fold_in(splits[1], 1), TOKENS // TOK_DEV)
    expert_ids_turns = jax.random.permutation(jax.random.fold_in(splits[1], 3), TOKENS // TOK_DEV)
    expert_ids = jax.vmap(lambda own, number: deal_out(jax.random.fold_in(splits[1], 2), own, number, TOK_DEV, EXPERTS, TOPK, CAP, 2))(expert_ids_keys, expert_ids_turns).reshape((TOKENS, TOPK))
    router_weight = normal_values(splits[2], (D, EXPERTS), D ** -0.5, 0.1875)
    gate_weight = normal_values(splits[3], (EXPERTS, D, FF), D ** -0.5, 0.1875, ((0, 32), (1, 16)))
    up_weight = normal_values(splits[4], (EXPERTS, D, FF), D ** -0.5, 0.1875, ((0, 32), (1, 16)))
    down_weight = normal_values(splits[5], (EXPERTS, FF, D), FF ** -0.5, 0.3125, ((0, 32), (2, 16)))
    grad_out = normal_values(splits[6], (TOKENS, D), 1.0, 6.0, ((0, 512),))
    return dict(tokens=tokens, expert_ids=expert_ids, router_weight=router_weight, gate_weight=gate_weight, up_weight=up_weight, down_weight=down_weight, grad_out=grad_out)


def route_slots(flat_ids, expert_count):
    hits = (flat_ids[:, None] == jnp.arange(expert_count, dtype=jnp.int32)[None, :]).astype(jnp.int32)
    before = jnp.cumsum(hits, axis=0) - hits
    return jnp.sum(before * hits, axis=1).astype(jnp.int32)


def expert_block(rows_in, grad_rows, w_gate, w_up, w_down):
    gate_act = jnp.dot(rows_in, w_gate, preferred_element_type=jnp.float32)
    up_act = jnp.dot(rows_in, w_up, preferred_element_type=jnp.float32)
    hidden = (jax.nn.silu(gate_act) * up_act).astype(jnp.bfloat16)
    produced = jnp.dot(hidden, w_down, preferred_element_type=jnp.float32).astype(jnp.bfloat16)
    contract = (((1,), (1,)), ((), ()))
    grad_hidden = lax.dot_general(grad_rows, w_down, contract, preferred_element_type=jnp.float32)
    sigma = jax.nn.sigmoid(gate_act)
    grad_gate = (grad_hidden * up_act * sigma * (1.0 + gate_act * (1.0 - sigma))).astype(jnp.bfloat16)
    grad_up = (grad_hidden * gate_act * sigma).astype(jnp.bfloat16)
    returned = lax.dot_general(grad_gate, w_gate, contract, preferred_element_type=jnp.float32)
    returned = returned + lax.dot_general(grad_up, w_up, contract, preferred_element_type=jnp.float32)
    return produced, returned.astype(jnp.bfloat16)


def reference(tokens, expert_ids, router_weight, gate_weight, up_weight, down_weight, grad_out):
    total = tokens.shape[0]
    feature_dim = tokens.shape[1]
    blocks = total // TOK_DEV
    slot_rows = blocks * CAP
    logits = jnp.dot(tokens, router_weight, preferred_element_type=jnp.float32)
    chosen = jnp.take_along_axis(logits, expert_ids, axis=1)
    mixing = 1.0 / jnp.sum(jnp.exp(chosen[:, None, :] - chosen[:, :, None]), axis=2)
    slots = jax.vmap(route_slots, in_axes=(0, None))(expert_ids.reshape(blocks, TOK_DEV * TOPK), EXPERTS)
    slots = slots.reshape(total, TOPK)
    owner = (jnp.arange(total, dtype=jnp.int32) // TOK_DEV)[:, None]
    position = (owner * CAP + slots).astype(jnp.int32)
    scaled_grad = (mixing[:, :, None] * grad_out.astype(jnp.float32)[:, None, :]).astype(jnp.bfloat16)

    def one_expert(running, inputs):
        out_rows, back_rows = running
        expert, w_gate, w_up, w_down = inputs
        mine = expert_ids == expert
        target = jnp.where(mine, position, slot_rows).astype(jnp.int32)
        sent = jnp.zeros((slot_rows, feature_dim), jnp.bfloat16)
        sent_grad = jnp.zeros((slot_rows, feature_dim), jnp.bfloat16)
        for member in range(TOPK):
            sent = sent.at[target[:, member]].set(tokens, mode="drop")
            sent_grad = sent_grad.at[target[:, member]].set(scaled_grad[:, member], mode="drop")
        produced, returned = expert_block(sent, sent_grad, w_gate, w_up, w_down)
        fetch = jnp.minimum(target, slot_rows - 1).astype(jnp.int32)
        for member in range(TOPK):
            picked = jnp.take(produced, fetch[:, member], axis=0)
            out_rows = out_rows.at[:, member].set(jnp.where(mine[:, member, None], picked, out_rows[:, member]))
            picked_back = jnp.take(returned, fetch[:, member], axis=0)
            back_rows = back_rows.at[:, member].set(jnp.where(mine[:, member, None], picked_back, back_rows[:, member]))
        return (out_rows, back_rows), None

    start = (jnp.zeros((total, TOPK, feature_dim), jnp.bfloat16), jnp.zeros((total, TOPK, feature_dim), jnp.bfloat16))
    (out_rows, back_rows), _ = lax.scan(one_expert, start, (jnp.arange(EXPERTS, dtype=jnp.int32), gate_weight, up_weight, down_weight))
    out_float = out_rows.astype(jnp.float32)
    moe_out = jnp.sum(mixing[:, :, None] * out_float, axis=1).astype(jnp.bfloat16)
    scores = jnp.einsum("td,tkd->tk", grad_out.astype(jnp.float32), out_float)
    dlogit = mixing * (scores - jnp.sum(mixing * scores, axis=1, keepdims=True))
    onehot = (expert_ids[:, :, None] == jnp.arange(EXPERTS, dtype=jnp.int32)[None, None, :]).astype(jnp.float32)
    dense = jnp.sum(onehot * dlogit[:, :, None], axis=1).astype(jnp.bfloat16)
    router_back = lax.dot_general(dense, router_weight, (((1,), (1,)), ((), ())), preferred_element_type=jnp.float32)
    grad_tokens = (jnp.sum(back_rows.astype(jnp.float32), axis=1) + router_back).astype(jnp.bfloat16)
    router_grad = lax.dot_general(tokens, dense, (((0,), (0,)), ((), ())), preferred_element_type=jnp.float32)
    return moe_out, grad_tokens, router_grad
```

```python
import functools

import jax
import jax.numpy as jnp
from jax import lax
from jax.experimental import pallas as pl
from jax.experimental.pallas import tpu as pltpu
from jax.sharding import PartitionSpec as P

MESH = pl.DeviceIdType.MESH
F32 = jnp.float32
BF16 = jnp.bfloat16
ROWS = 16
CAP = 12
LANES = 128


def iota(shape, dim):
    return lax.broadcasted_iota(jnp.int32, shape, dim)


def mm(a, b):
    return lax.dot_general(a, b, (((1,), (0,)), ((), ())), preferred_element_type=F32)


def mm_t(a, b):
    return lax.dot_general(a, b, (((1,), (1,)), ((), ())), preferred_element_type=F32)


def kernel(
    sizes,
    tok_ref, ids_ref, rw_ref, wg_ref, wu_ref, wd_ref, g_ref,
    moe_ref, gt_ref, rg_ref,
    sx, sg, rx, rg, px, pg, cx, cg, act, up, w, part, r1, ax, ay, fin,
    s_in, r_in, s_out, r_out, s_ring, r_ring, s_pair, r_pair, s_ar, r_ar,
):
    dpn, tpn, cpn = sizes
    groups = tpn * cpn
    half = groups // 2
    nx = cpn // 2
    nz = dpn // 2
    t_count, d = tok_ref.shape
    q = d // 4
    dp = lax.axis_index("dp")
    tp = lax.axis_index("tp")
    cp = lax.axis_index("cp")
    me = tp * cpn + cp
    xi = lax.rem(cp, nx)
    yh = cp // nx
    z = dp // 2
    core = lax.rem(dp, 2)

    def peer(r):
        to_tp = lax.rem(tp + lax.rem(r // nx, tpn), tpn)
        to_cp = lax.rem(yh + r // half, 2) * nx + lax.rem(xi + lax.rem(r, nx), nx)
        return to_tp, to_cp

    def mirror(r):
        back_x = lax.rem(nx - lax.rem(r, nx), nx)
        back_tp = lax.rem(tpn - lax.rem(r // nx, tpn), tpn)
        return (r // half) * half + back_tp * nx + back_x

    def remote(src, dst, send, recv, device):
        return pltpu.make_async_remote_copy(
            src_ref=src, dst_ref=dst, send_sem=send, recv_sem=recv,
            device_id=device, device_id_type=MESH,
        )

    def wait_bytes(ref, sem):
        pltpu.make_async_copy(ref, ref, sem).wait()

    barrier = pltpu.get_barrier_semaphore()

    def greet_plane(r, carry):
        to_tp, to_cp = peer(r)
        pl.semaphore_signal(barrier, inc=1, device_id=(dp, to_tp, to_cp), device_id_type=MESH)
        return carry

    def greet_dp(o, carry):
        pl.semaphore_signal(
            barrier, inc=1, device_id=(lax.rem(dp + o, dpn), tp, cp), device_id_type=MESH
        )
        return carry

    lax.fori_loop(1, groups, greet_plane, 0)
    lax.fori_loop(1, dpn, greet_dp, 0)

    tokens = tok_ref[...]
    grads = g_ref[...]
    lane = iota((t_count, LANES), 1)
    hot = [(lane == ids_ref[:, k : k + 1]).astype(F32) for k in range(2)]
    both = hot[0] + hot[1]
    both_t = both.T.astype(BF16)
    upper = (iota((t_count, t_count), 0) < iota((t_count, t_count), 1)).astype(BF16)
    before_t = mm(both_t, upper).astype(BF16)
    span = groups * ROWS
    spread_t = (iota((span, LANES), 0) // ROWS == iota((span, LANES), 1)).astype(BF16)
    slot_t = mm(spread_t, before_t)
    named_t = mm(spread_t, both_t) > 0.5
    row_t = lax.rem(iota((span, t_count), 0), ROWS)

    def choice(named, slot, row, j):
        wanted = row if j is None else jnp.where(row >= CAP, 3 * (row - CAP) + j, -1)
        return (named & (slot == wanted.astype(F32))).astype(BF16)

    main_t = choice(named_t, slot_t, row_t, None)
    tail_t = [choice(named_t, slot_t, row_t, j) for j in range(3)]

    def pack_home(values, out):
        for j in range(3):
            piece = mm(main_t, values[:, q * j : q * (j + 1)]) + mm(tail_t[j], values[:, 3 * q :])
            out[:, :, q * j : q * (j + 1)] = piece.astype(BF16).reshape(groups, ROWS, q)

    pack_home(tokens, sx)
    pack_home(grads, sg)

    shard = wg_ref.shape[1]
    eye = (iota((shard, shard), 0) == iota((shard, shard), 1)).astype(BF16)
    w[dp, 0] = wg_ref[0]
    w[dp, 1] = wu_ref[0]
    w[dp, 2] = mm_t(eye, wd_ref[0]).astype(BF16)

    pl.semaphore_wait(barrier, groups - 1 + dpn - 1)

    def ring(step, sign):
        slot = lax.rem(z - sign * step + nz, nz) * 2 + core
        index = step if sign > 0 else nz // 2 + step
        return remote(
            w.at[slot], w.at[slot], s_ring.at[index], r_ring.at[index],
            (lax.rem(z + sign + nz, nz) * 2 + core, tp, cp),
        )

    def pair(index, shift):
        slot = lax.rem(z + shift + nz, nz) * 2 + core
        return remote(
            w.at[slot], w.at[slot], s_pair.at[index], r_pair.at[index],
            (z * 2 + 1 - core, tp, cp),
        )

    rights, lefts = nz // 2, nz // 2 - 1
    right = [ring(s, 1) for s in range(rights)]
    left = [ring(s, -1) for s in range(lefts)]
    pairs = [pair(0, 0)]
    right[0].start()
    if lefts:
        left[0].start()
    pairs[0].start()

    def send_in(src, dst, phase):
        for h in range(2):
            def one(r, carry):
                to_tp, to_cp = peer(r)
                remote(
                    src.at[to_tp * cpn + to_cp], dst.at[mirror(r)],
                    s_in.at[2 * phase + h], r_in.at[2 * phase + h], (dp, to_tp, to_cp),
                ).start()
                return carry

            lax.fori_loop(max(1, half * h), half * (h + 1), one, 0)

    send_in(sx, rx, 0)
    send_in(sg, rg, 1)
    rx[0] = sx[me]
    rg[0] = sg[me]

    logits = mm(tokens, rw_ref[...])
    ecount = rw_ref.shape[1]
    chosen = [jnp.sum(logits * hot[k][:, :ecount], axis=1, keepdims=True) for k in range(2)]
    mixing = [
        1.0 / (1.0 + jnp.exp(chosen[1] - chosen[0])),
        1.0 / (1.0 + jnp.exp(chosen[0] - chosen[1])),
    ]
    lower = (iota((t_count, t_count), 1) < iota((t_count, t_count), 0)).astype(BF16)
    before = mm(lower, both.astype(BF16)).astype(BF16)
    spread = (iota((LANES, span), 1) // ROWS == iota((LANES, span), 0)).astype(BF16)
    slot = mm(before, spread)
    row = lax.rem(iota((t_count, span), 1), ROWS)
    picks = []
    for k in range(2):
        named = mm(hot[k].astype(BF16), spread) > 0.5
        picks.append([choice(named, slot, row, None)] + [choice(named, slot, row, j) for j in range(3)])

    for s in range(rights):
        right[s].wait_recv()
        if s + 1 < rights:
            right[s + 1].start()
        copy = pair(len(pairs), -(s + 1))
        copy.start()
        pairs.append(copy)
        if s < lefts:
            left[s].wait_recv()
            if s + 1 < lefts:
                left[s + 1].start()
            copy = pair(len(pairs), s + 1)
            copy.start()
            pairs.append(copy)
    for copy in pairs:
        copy.wait_recv()

    size = half * ROWS
    pr, qr = iota((size, size), 0), iota((size, size), 1)
    same = pr // ROWS == qr // ROWS
    pr, qr = lax.rem(pr, ROWS), lax.rem(qr, ROWS)
    unpack = [
        (same & (pr < CAP) & (qr >= CAP) & (pr == 3 * (qr - CAP) + j)).astype(BF16) for j in range(3)
    ]
    repack = [
        (same & (qr < CAP) & (pr >= CAP) & (qr == 3 * (pr - CAP) + j)).astype(BF16) for j in range(3)
    ]
    is_main = lax.rem(iota((size, q), 0), ROWS) < CAP

    def open_rows(ref, h):
        packed = ref[half * h : half * (h + 1)].reshape(size, 3 * q)
        tail = sum(mm(unpack[j], packed[:, q * j : q * (j + 1)]) for j in range(3))
        return jnp.concatenate([packed, tail.astype(BF16)], axis=1)

    def close_rows(values, ref, h):
        for j in range(3):
            piece = jnp.where(
                is_main, values[:, q * j : q * (j + 1)].astype(F32), mm(repack[j], values[:, 3 * q :])
            )
            ref[half * h : half * (h + 1), :, q * j : q * (j + 1)] = piece.astype(BF16).reshape(
                half, ROWS, q
            )

    def weight(i):
        return w[:, i].reshape(d, w.shape[3])

    def wait_in(ref, phase, h):
        lo = max(1, half * h)
        wait_bytes(ref.at[pl.ds(lo, half * (h + 1) - lo)], r_in.at[2 * phase + h])

    def send_out(src, dst, phase, h):
        def one(r, carry):
            to_tp, to_cp = peer(r)
            remote(
                src.at[r], dst.at[me], s_out.at[2 * phase + h], r_out.at[phase],
                (dp, to_tp, to_cp),
            ).start()
            return carry

        lax.fori_loop(max(1, half * h), half * (h + 1), one, 0)

    for h in range(2):
        wait_in(rx, 0, h)
        rows = open_rows(rx, h)
        gate = mm(rows, weight(0))
        upper_act = mm(rows, weight(1))
        act[size * h : size * (h + 1)] = gate
        up[size * h : size * (h + 1)] = upper_act
        hidden = (gate * jax.nn.sigmoid(gate) * upper_act).astype(BF16)
        close_rows(mm_t(hidden, weight(2)).astype(BF16), px, h)
        send_out(px, cx, 0, h)
    cx[me] = px[0]
    for h in range(2):
        wait_in(rg, 1, h)
        rows = open_rows(rg, h)
        grad_hidden = mm(rows, weight(2))
        gate = act[size * h : size * (h + 1)]
        upper_act = up[size * h : size * (h + 1)]
        sigma = jax.nn.sigmoid(gate)
        grad_gate = (grad_hidden * upper_act * sigma * (1.0 + gate * (1.0 - sigma))).astype(BF16)
        grad_up = (grad_hidden * gate * sigma).astype(BF16)
        back = mm_t(grad_gate, weight(0)) + mm_t(grad_up, weight(1))
        close_rows(back.astype(BF16), pg, h)
        send_out(pg, cg, 1, h)
    cg[me] = pg[0]

    def home_rows(ref, k):
        packed = ref[...].reshape(span, 3 * q)
        main = mm(picks[k][0], packed)
        tail = sum(mm(picks[k][1 + j], packed[:, q * j : q * (j + 1)]) for j in range(3))
        return jnp.concatenate([main, tail], axis=1)

    wait_bytes(cx.at[pl.ds(0, groups - 1)], r_out.at[0])
    grads32 = grads.astype(F32)
    total = None
    scores = []
    for k in range(2):
        rows = home_rows(cx, k)
        scores.append(jnp.sum(grads32 * rows, axis=1, keepdims=True))
        total = mixing[k] * rows if total is None else total + mixing[k] * rows
    moe_ref[...] = total.astype(BF16)
    mean = mixing[0] * scores[0] + mixing[1] * scores[1]
    dense = sum(hot[k] * (mixing[k] * (scores[k] - mean)) for k in range(2))
    dense_t = dense.T.astype(BF16)
    part[...] = mm(dense_t, tokens)[: part.shape[0]]

    cw = r1.shape[2]
    nb = d // cw

    def chunk(c):
        return pl.ds(pl.multiple_of(8 * (c // nb), 8), 8), pl.ds(
            pl.multiple_of(cw * lax.rem(c, nb), LANES), cw
        )

    def scatter(o, carry):
        to = lax.rem(dp + o, dpn)
        remote(part.at[chunk(to)], r1.at[o - 1], s_ar.at[0], r_ar.at[0], (to, tp, cp)).start()
        return carry

    lax.fori_loop(1, dpn, scatter, 0)

    router_back = mm_t(dense.astype(BF16)[:, :ecount], rw_ref[...])

    wait_bytes(r1, r_ar.at[0])
    rows_own, cols_own = chunk(dp)
    ax[xi] = jnp.sum(r1[...], axis=0) + part[rows_own, cols_own]
    for o in range(1, nx):
        remote(
            ax.at[xi], ax.at[xi], s_ar.at[1], r_ar.at[1],
            (dp, tp, yh * nx + lax.rem(xi + o, nx)),
        ).start()
    wait_bytes(ax.at[pl.ds(0, nx - 1)], r_ar.at[1])
    yn = 2 * tpn
    yi = yh * tpn + tp
    ay[yi] = jnp.sum(ax[...], axis=0)
    for o in range(1, yn):
        to = lax.rem(yi + o, yn)
        remote(
            ay.at[yi], ay.at[yi], s_ar.at[2], r_ar.at[2],
            (dp, lax.rem(to, tpn), (to // tpn) * nx + xi),
        ).start()
    wait_bytes(ay.at[pl.ds(0, yn - 1)], r_ar.at[2])
    fin[dp] = jnp.sum(ay[...], axis=0)

    def gather(o, carry):
        to = lax.rem(dp + o, dpn)
        remote(fin.at[dp], fin.at[dp], s_ar.at[3], r_ar.at[3], (to, tp, cp)).start()
        return carry

    lax.fori_loop(1, dpn, gather, 0)

    wait_bytes(cg.at[pl.ds(0, groups - 1)], r_out.at[1])
    gt_ref[...] = (
        mixing[0] * home_rows(cg, 0) + mixing[1] * home_rows(cg, 1) + router_back
    ).astype(BF16)

    wait_bytes(fin.at[pl.ds(0, dpn - 1)], r_ar.at[3])
    for c in range(dpn):
        rg_ref[8 * (c // nb) : 8 * (c // nb) + 8, cw * (c % nb) : cw * (c % nb + 1)] = fin[c]

    for phase, ref in enumerate((sx, sg)):
        for h in range(2):
            lo = max(1, half * h)
            wait_bytes(ref.at[pl.ds(lo, half * (h + 1) - lo)], s_in.at[2 * phase + h])
    for phase, ref in enumerate((px, pg)):
        for h in range(2):
            lo = max(1, half * h)
            wait_bytes(ref.at[pl.ds(lo, half * (h + 1) - lo)], s_out.at[2 * phase + h])
    for copy in right + left + pairs:
        copy.wait_send()
    wait_bytes(r1, s_ar.at[0])
    wait_bytes(ax.at[pl.ds(0, nx - 1)], s_ar.at[1])
    wait_bytes(ay.at[pl.ds(0, yn - 1)], s_ar.at[2])
    wait_bytes(fin.at[pl.ds(0, dpn - 1)], s_ar.at[3])


def on_device(tokens, expert_ids, router_weight, gate_weight, up_weight, down_weight, grad_out):
    sizes = tuple(lax.axis_size(name) for name in ("dp", "tp", "cp"))
    dpn, tpn, cpn = sizes
    groups = tpn * cpn
    t_count, d = tokens.shape
    shard, ff = gate_weight.shape[1:]
    block = pltpu.VMEM((groups, ROWS, 3 * d // 4), BF16)
    wide = 4 * d // dpn
    vmem = pl.BlockSpec(memory_space=pltpu.VMEM)
    dma = pltpu.SemaphoreType.DMA
    nz = dpn // 2
    moe, grad_tokens, router = pl.pallas_call(
        functools.partial(kernel, sizes),
        out_shape=(
            jax.ShapeDtypeStruct((t_count, d), BF16),
            jax.ShapeDtypeStruct((t_count, d), BF16),
            jax.ShapeDtypeStruct((32, d), F32),
        ),
        in_specs=[vmem] * 7,
        out_specs=(vmem,) * 3,
        scratch_shapes=[block] * 8
        + [
            pltpu.VMEM((groups * ROWS, ff), F32),
            pltpu.VMEM((groups * ROWS, ff), F32),
            pltpu.VMEM((dpn, 3, shard, ff), BF16),
            pltpu.VMEM((32, d), F32),
            pltpu.VMEM((dpn - 1, 8, wide), F32),
            pltpu.VMEM((cpn // 2, 8, wide), F32),
            pltpu.VMEM((2 * tpn, 8, wide), F32),
            pltpu.VMEM((dpn, 8, wide), F32),
            dma((4,)), dma((4,)), dma((4,)), dma((2,)),
            dma((nz - 1,)), dma((nz - 1,)), dma((nz,)), dma((nz,)),
            dma((4,)), dma((4,)),
        ],
        compiler_params=pltpu.CompilerParams(collective_id=0, has_side_effects=True),
        name="experts",
    )(tokens, expert_ids, router_weight, gate_weight, up_weight, down_weight, grad_out)
    return moe, grad_tokens, router[: router_weight.shape[1]].T


def solution(mesh):
    in_specs = (
        P(("dp", "tp", "cp"), None),
        P(("dp", "tp", "cp"), None),
        P(),
        P(("tp", "cp"), "dp", None),
        P(("tp", "cp"), "dp", None),
        P(("tp", "cp"), None, "dp"),
        P(("dp", "tp", "cp"), None),
    )
    out_specs = (P(("dp", "tp", "cp"), None), P(("dp", "tp", "cp"), None), P())
    return jax.shard_map(
        on_device, mesh=mesh, in_specs=in_specs, out_specs=out_specs, check_vma=False
    )
```

```python
import functools

import jax
import jax.numpy as jnp
from jax import lax
from jax.experimental import pallas as pl
from jax.experimental.pallas import tpu as pltpu
from jax.sharding import PartitionSpec as P

MESH = pl.DeviceIdType.MESH
F32 = jnp.float32
BF16 = jnp.bfloat16
ROWS = 16
CAP = 12
LANES = 128


def iota(shape, dim):
    return lax.broadcasted_iota(jnp.int32, shape, dim)


def mm(a, b):
    return lax.dot_general(a, b, (((1,), (0,)), ((), ())), preferred_element_type=F32)


def mm_t(a, b):
    return lax.dot_general(a, b, (((1,), (1,)), ((), ())), preferred_element_type=F32)


def kernel(
    sizes,
    tok_ref, ids_ref, rw_ref, wg_ref, wu_ref, wd_ref, g_ref,
    moe_ref, gt_ref, rg_ref,
    sx, sg, rx, rg, px, pg, cx, cg, act, up, ws, w, part, r1, ax, ay, fin,
    s_in, r_in, s_out, r_out, s_ring, r_ring, s_far, s_pair, r_own, s_ar, r_ar,
):
    dpn, tpn, cpn = sizes
    groups = tpn * cpn
    half = groups // 2
    nx = cpn // 2
    nz = dpn // 2
    t_count, d = tok_ref.shape
    q = d // 4
    dp = lax.axis_index("dp")
    tp = lax.axis_index("tp")
    cp = lax.axis_index("cp")
    xi = lax.rem(cp, nx)
    yh = cp // nx
    yn = 2 * tpn
    y = yh * tpn + tp
    z = dp // 2
    core = lax.rem(dp, 2)
    mine = tp * cpn + core * nx + xi

    def shift(dl, h):
        return dl - tpn * ((2 * dl + h) // (tpn + 1))

    def split(r):
        return r // (2 * nx), lax.rem(r // 2, nx), lax.rem(r, 2)

    def device(to_y, to_x, to_core):
        return z * 2 + to_core, lax.rem(to_y, tpn), (to_y // tpn) * nx + to_x

    def host(r):
        dl, dx, dc = split(r)
        h = lax.rem(core + dc, 2)
        to_x = lax.rem(xi + dx, nx)
        expert = lax.rem(tp + dl, tpn) * cpn + h * nx + to_x
        return expert, device(lax.rem(y + shift(dl, h) + yn, yn), to_x, h)

    def home(r):
        dl, dx, dc = split(r)
        return device(
            lax.rem(y - shift(dl, core) + yn, yn), lax.rem(xi - dx + nx, nx), lax.rem(core - dc + 2, 2)
        )

    def remote(src, dst, send, recv, device):
        return pltpu.make_async_remote_copy(
            src_ref=src, dst_ref=dst, send_sem=send, recv_sem=recv,
            device_id=device, device_id_type=MESH,
        )

    def wait_bytes(ref, sem):
        pltpu.make_async_copy(ref, ref, sem).wait()

    barrier = pltpu.get_barrier_semaphore()

    def greet(to):
        pl.semaphore_signal(barrier, inc=1, device_id=to, device_id_type=MESH)

    def greet_plane(r, carry):
        dy, rest = r // (2 * nx), lax.rem(r, 2 * nx)
        greet(device(lax.rem(y + dy, yn), lax.rem(xi + rest // 2, nx), lax.rem(core + rest, 2)))
        return carry

    def greet_dp(o, carry):
        greet((lax.rem(z + o // 2, nz) * 2 + lax.rem(o, 2), tp, cp))
        return carry

    lax.fori_loop(1, 2 * groups, greet_plane, 0)
    lax.fori_loop(2, dpn, greet_dp, 0)

    tokens = tok_ref[...]
    grads = g_ref[...]
    lane = iota((t_count, LANES), 1)
    hot = [(lane == ids_ref[:, k : k + 1]).astype(F32) for k in range(2)]
    both = hot[0] + hot[1]
    both_t = both.T.astype(BF16)
    upper = (iota((t_count, t_count), 0) < iota((t_count, t_count), 1)).astype(BF16)
    before_t = mm(both_t, upper).astype(BF16)
    span = groups * ROWS
    spread_t = (iota((span, LANES), 0) // ROWS == iota((span, LANES), 1)).astype(BF16)
    slot_t = mm(spread_t, before_t)
    named_t = mm(spread_t, both_t) > 0.5
    row_t = lax.rem(iota((span, t_count), 0), ROWS)

    def choice(named, slot, row, j):
        wanted = row if j is None else jnp.where(row >= CAP, 3 * (row - CAP) + j, -1)
        return (named & (slot == wanted.astype(F32))).astype(BF16)

    main_t = choice(named_t, slot_t, row_t, None)
    tail_t = [choice(named_t, slot_t, row_t, j) for j in range(3)]

    def pack_home(values, out):
        for j in range(3):
            piece = mm(main_t, values[:, q * j : q * (j + 1)]) + mm(tail_t[j], values[:, 3 * q :])
            out[:, :, q * j : q * (j + 1)] = piece.astype(BF16).reshape(groups, ROWS, q)

    pack_home(tokens, sx)
    pack_home(grads, sg)

    shard = wg_ref.shape[1]
    eye = (iota((shard, shard), 0) == iota((shard, shard), 1)).astype(BF16)
    shards = [wg_ref[0], wu_ref[0], mm_t(eye, wd_ref[0]).astype(BF16)]
    for i in range(3):
        ws[i] = shards[i]

    @pl.when(core == yh)
    def _():
        for i in range(3):
            w[i, dp] = shards[i]

    pl.semaphore_wait(barrier, 2 * groups - 1 + dpn - 2)

    def far(i):
        return remote(
            ws.at[i], w.at[i, dp], s_far.at[i], r_own.at[i],
            (z * 2 + yh, tp, (1 - yh) * nx + xi),
        )

    def pair(i):
        return remote(
            ws.at[i], w.at[i, dp], s_pair.at[i], r_own.at[i], (z * 2 + 1 - core, tp, cp)
        )

    for i in range(3):
        far(i).start()

    @pl.when(core != yh)
    def _():
        for i in range(3):
            pair(i).start()

    def send_in(src, dst, phase):
        for h in range(2):
            def one(r, carry):
                expert, to = host(r)
                remote(
                    src.at[expert], dst.at[r], s_in.at[2 * phase + h], r_in.at[2 * phase + h], to
                ).start()
                return carry

            lax.fori_loop(max(1, half * h), half * (h + 1), one, 0)

    send_in(sx, rx, 0)
    send_in(sg, rg, 1)
    rx[0] = sx[mine]
    rg[0] = sg[mine]

    steps = nz // 2

    def ring(sign, step, i):
        at = pl.ds(lax.rem(z - sign * step + nz, nz) * 2, 2)
        index = ((0 if sign > 0 else steps) + step) * 3 + i
        return remote(
            w.at[i, at], w.at[i, at], s_ring.at[index], r_ring.at[index],
            (lax.rem(z + sign + nz, nz) * 2 + core, tp, cp),
        )

    links = {}
    for sign in (1, -1):
        for s in range(steps):
            for i in range(3):
                if s + 1 < steps or (i == 1) == (sign < 0):
                    links[sign, s, i] = ring(sign, s, i)

    for i in range(3):
        @pl.when(core == yh)
        def _():
            wait_bytes(w.at[i, pl.ds(0, 1)], r_own.at[i])

        @pl.when(core != yh)
        def _():
            wait_bytes(w.at[i, pl.ds(0, 2)], r_own.at[i])

        for sign in (1, -1):
            if (sign, 0, i) in links:
                links[sign, 0, i].start()

    logits = mm(tokens, rw_ref[...])
    ecount = rw_ref.shape[1]
    chosen = [jnp.sum(logits * hot[k][:, :ecount], axis=1, keepdims=True) for k in range(2)]
    mixing = [
        1.0 / (1.0 + jnp.exp(chosen[1] - chosen[0])),
        1.0 / (1.0 + jnp.exp(chosen[0] - chosen[1])),
    ]
    lower = (iota((t_count, t_count), 1) < iota((t_count, t_count), 0)).astype(BF16)
    before = mm(lower, both.astype(BF16)).astype(BF16)
    spread = (iota((LANES, span), 1) // ROWS == iota((LANES, span), 0)).astype(BF16)
    slot = mm(before, spread)
    row = lax.rem(iota((t_count, span), 1), ROWS)
    picks = []
    for k in range(2):
        named = mm(hot[k].astype(BF16), spread) > 0.5
        picks.append([choice(named, slot, row, None)] + [choice(named, slot, row, j) for j in range(3)])

    for s in range(steps):
        for i in range(3):
            for sign in (1, -1):
                if (sign, s, i) in links:
                    links[sign, s, i].wait_recv()
                if (sign, s + 1, i) in links:
                    links[sign, s + 1, i].start()

    size = half * ROWS
    pr, qr = iota((size, size), 0), iota((size, size), 1)
    same = pr // ROWS == qr // ROWS
    pr, qr = lax.rem(pr, ROWS), lax.rem(qr, ROWS)
    unpack = [
        (same & (pr < CAP) & (qr >= CAP) & (pr == 3 * (qr - CAP) + j)).astype(BF16) for j in range(3)
    ]
    repack = [
        (same & (qr < CAP) & (pr >= CAP) & (qr == 3 * (pr - CAP) + j)).astype(BF16) for j in range(3)
    ]
    is_main = lax.rem(iota((size, q), 0), ROWS) < CAP

    def open_rows(ref, h):
        packed = ref[half * h : half * (h + 1)].reshape(size, 3 * q)
        tail = sum(mm(unpack[j], packed[:, q * j : q * (j + 1)]) for j in range(3))
        return jnp.concatenate([packed, tail.astype(BF16)], axis=1)

    def close_rows(values, ref, h):
        for j in range(3):
            piece = jnp.where(
                is_main, values[:, q * j : q * (j + 1)].astype(F32), mm(repack[j], values[:, 3 * q :])
            )
            ref[half * h : half * (h + 1), :, q * j : q * (j + 1)] = piece.astype(BF16).reshape(
                half, ROWS, q
            )

    def weight(i):
        return w[i].reshape(d, w.shape[3])

    def wait_in(ref, phase, h):
        lo = max(1, half * h)
        wait_bytes(ref.at[pl.ds(lo, half * (h + 1) - lo)], r_in.at[2 * phase + h])

    def send_out(src, dst, phase, h):
        def one(r, carry):
            remote(
                src.at[r], dst.at[mine], s_out.at[2 * phase + h], r_out.at[phase], home(r)
            ).start()
            return carry

        lax.fori_loop(max(1, half * h), half * (h + 1), one, 0)

    for h in range(2):
        wait_in(rx, 0, h)
        rows = open_rows(rx, h)
        gate = mm(rows, weight(0))
        upper_act = mm(rows, weight(1))
        act[size * h : size * (h + 1)] = gate
        up[size * h : size * (h + 1)] = upper_act
        hidden = (gate * jax.nn.sigmoid(gate) * upper_act).astype(BF16)
        close_rows(mm_t(hidden, weight(2)).astype(BF16), px, h)
        send_out(px, cx, 0, h)
    cx[mine] = px[0]
    for h in range(2):
        wait_in(rg, 1, h)
        rows = open_rows(rg, h)
        grad_hidden = mm(rows, weight(2))
        gate = act[size * h : size * (h + 1)]
        upper_act = up[size * h : size * (h + 1)]
        sigma = jax.nn.sigmoid(gate)
        grad_gate = (grad_hidden * upper_act * sigma * (1.0 + gate * (1.0 - sigma))).astype(BF16)
        grad_up = (grad_hidden * gate * sigma).astype(BF16)
        back = mm_t(grad_gate, weight(0)) + mm_t(grad_up, weight(1))
        close_rows(back.astype(BF16), pg, h)
        send_out(pg, cg, 1, h)
    cg[mine] = pg[0]

    def home_rows(ref, k):
        packed = ref[...].reshape(span, 3 * q)
        main = mm(picks[k][0], packed)
        tail = sum(mm(picks[k][1 + j], packed[:, q * j : q * (j + 1)]) for j in range(3))
        return jnp.concatenate([main, tail], axis=1)

    wait_bytes(cx.at[pl.ds(0, groups - 1)], r_out.at[0])
    grads32 = grads.astype(F32)
    total = None
    scores = []
    for k in range(2):
        rows = home_rows(cx, k)
        scores.append(jnp.sum(grads32 * rows, axis=1, keepdims=True))
        total = mixing[k] * rows if total is None else total + mixing[k] * rows
    moe_ref[...] = total.astype(BF16)
    mean = mixing[0] * scores[0] + mixing[1] * scores[1]
    dense = sum(hot[k] * (mixing[k] * (scores[k] - mean)) for k in range(2))
    dense_t = dense.T.astype(BF16)
    part[...] = mm(dense_t, tokens)[: part.shape[0]]

    cw = r1.shape[2]
    nb = d // cw

    def chunk(c):
        return pl.ds(pl.multiple_of(8 * (c // nb), 8), 8), pl.ds(
            pl.multiple_of(cw * lax.rem(c, nb), LANES), cw
        )

    def scatter(o, carry):
        to = lax.rem(dp + o, dpn)
        remote(part.at[chunk(to)], r1.at[o - 1], s_ar.at[0], r_ar.at[0], (to, tp, cp)).start()
        return carry

    lax.fori_loop(1, dpn, scatter, 0)

    router_back = mm_t(dense.astype(BF16)[:, :ecount], rw_ref[...])

    wait_bytes(r1, r_ar.at[0])
    rows_own, cols_own = chunk(dp)
    ax[xi] = jnp.sum(r1[...], axis=0) + part[rows_own, cols_own]
    for o in range(1, nx):
        remote(
            ax.at[xi], ax.at[xi], s_ar.at[1], r_ar.at[1],
            (dp, tp, yh * nx + lax.rem(xi + o, nx)),
        ).start()
    wait_bytes(ax.at[pl.ds(0, nx - 1)], r_ar.at[1])
    ay[y] = jnp.sum(ax[...], axis=0)
    for o in range(1, yn):
        to = lax.rem(y + o, yn)
        remote(
            ay.at[y], ay.at[y], s_ar.at[2], r_ar.at[2],
            (dp, lax.rem(to, tpn), (to // tpn) * nx + xi),
        ).start()
    wait_bytes(ay.at[pl.ds(0, yn - 1)], r_ar.at[2])
    fin[dp] = jnp.sum(ay[...], axis=0)

    def gather(o, carry):
        to = lax.rem(dp + o, dpn)
        remote(fin.at[dp], fin.at[dp], s_ar.at[3], r_ar.at[3], (to, tp, cp)).start()
        return carry

    lax.fori_loop(1, dpn, gather, 0)

    wait_bytes(cg.at[pl.ds(0, groups - 1)], r_out.at[1])
    gt_ref[...] = (
        mixing[0] * home_rows(cg, 0) + mixing[1] * home_rows(cg, 1) + router_back
    ).astype(BF16)

    wait_bytes(fin.at[pl.ds(0, dpn - 1)], r_ar.at[3])
    for c in range(dpn):
        rg_ref[8 * (c // nb) : 8 * (c // nb) + 8, cw * (c % nb) : cw * (c % nb + 1)] = fin[c]

    for phase, ref in enumerate((sx, sg)):
        for h in range(2):
            lo = max(1, half * h)
            wait_bytes(ref.at[pl.ds(lo, half * (h + 1) - lo)], s_in.at[2 * phase + h])
    for phase, ref in enumerate((px, pg)):
        for h in range(2):
            lo = max(1, half * h)
            wait_bytes(ref.at[pl.ds(lo, half * (h + 1) - lo)], s_out.at[2 * phase + h])
    for i in range(3):
        far(i).wait_send()

    @pl.when(core != yh)
    def _():
        for i in range(3):
            pair(i).wait_send()

    for copy in links.values():
        copy.wait_send()
    wait_bytes(r1, s_ar.at[0])
    wait_bytes(ax.at[pl.ds(0, nx - 1)], s_ar.at[1])
    wait_bytes(ay.at[pl.ds(0, yn - 1)], s_ar.at[2])
    wait_bytes(fin.at[pl.ds(0, dpn - 1)], s_ar.at[3])


def on_device(tokens, expert_ids, router_weight, gate_weight, up_weight, down_weight, grad_out):
    sizes = tuple(lax.axis_size(name) for name in ("dp", "tp", "cp"))
    dpn, tpn, cpn = sizes
    groups = tpn * cpn
    t_count, d = tokens.shape
    shard, ff = gate_weight.shape[1:]
    block = pltpu.VMEM((groups, ROWS, 3 * d // 4), BF16)
    wide = 4 * d // dpn
    vmem = pl.BlockSpec(memory_space=pltpu.VMEM)
    dma = pltpu.SemaphoreType.DMA
    nz = dpn // 2
    moe, grad_tokens, router = pl.pallas_call(
        functools.partial(kernel, sizes),
        out_shape=(
            jax.ShapeDtypeStruct((t_count, d), BF16),
            jax.ShapeDtypeStruct((t_count, d), BF16),
            jax.ShapeDtypeStruct((32, d), F32),
        ),
        in_specs=[vmem] * 7,
        out_specs=(vmem,) * 3,
        scratch_shapes=[block] * 8
        + [
            pltpu.VMEM((groups * ROWS, ff), F32),
            pltpu.VMEM((groups * ROWS, ff), F32),
            pltpu.VMEM((3, shard, ff), BF16),
            pltpu.VMEM((3, dpn, shard, ff), BF16),
            pltpu.VMEM((32, d), F32),
            pltpu.VMEM((dpn - 1, 8, wide), F32),
            pltpu.VMEM((cpn // 2, 8, wide), F32),
            pltpu.VMEM((2 * tpn, 8, wide), F32),
            pltpu.VMEM((dpn, 8, wide), F32),
            dma((4,)), dma((4,)), dma((4,)), dma((2,)),
            dma((3 * nz,)), dma((3 * nz,)), dma((3,)), dma((3,)), dma((3,)),
            dma((4,)), dma((4,)),
        ],
        compiler_params=pltpu.CompilerParams(collective_id=0, has_side_effects=True),
        name="experts",
    )(tokens, expert_ids, router_weight, gate_weight, up_weight, down_weight, grad_out)
    return moe, grad_tokens, router[: router_weight.shape[1]].T


def solution(mesh):
    in_specs = (
        P(("dp", "tp", "cp"), None),
        P(("dp", "tp", "cp"), None),
        P(),
        P(("tp", "cp"), "dp", None),
        P(("tp", "cp"), "dp", None),
        P(("tp", "cp"), None, "dp"),
        P(("dp", "tp", "cp"), None),
    )
    out_specs = (P(("dp", "tp", "cp"), None), P(("dp", "tp", "cp"), None), P())
    return jax.shard_map(
        on_device, mesh=mesh, in_specs=in_specs, out_specs=out_specs, check_vma=False
    )
```

```python
import functools

import jax
import jax.numpy as jnp
from jax import lax
from jax.experimental import pallas as pl
from jax.experimental.pallas import tpu as pltpu
from jax.sharding import PartitionSpec as P

MESH = pl.DeviceIdType.MESH
F32 = jnp.float32
BF16 = jnp.bfloat16
ROWS = 16
CAP = 12
LANES = 128


def iota(shape, dim):
    return lax.broadcasted_iota(jnp.int32, shape, dim)


def mm(a, b):
    return lax.dot_general(a, b, (((1,), (0,)), ((), ())), preferred_element_type=F32)


def mm_t(a, b):
    return lax.dot_general(a, b, (((1,), (1,)), ((), ())), preferred_element_type=F32)


def kernel(
    sizes,
    tok_ref, ids_ref, rw_ref, wg_ref, wu_ref, wd_ref, g_ref,
    moe_ref, gt_ref, rg_ref,
    sx, sg, rx, rg, px, pg, cx, cg, xs, gs, act, up, ws, w, part, r1, ax, ay, fin,
    s_in, r_in, s_out, r_out, s_ring, r_ring, s_far, s_pair, r_own, s_ar, r_ar,
):
    dpn, tpn, cpn = sizes
    groups = tpn * cpn
    half = groups // 2
    nx = cpn // 2
    nz = dpn // 2
    t_count, d = tok_ref.shape
    q = d // 4
    dp = lax.axis_index("dp")
    tp = lax.axis_index("tp")
    cp = lax.axis_index("cp")
    xi = lax.rem(cp, nx)
    yh = cp // nx
    yn = 2 * tpn
    y = yh * tpn + tp
    z = dp // 2
    core = lax.rem(dp, 2)
    mine = tp * cpn + core * nx + xi

    def shift(dl, h):
        return dl - tpn * ((2 * dl + h) // (tpn + 1))

    def split(r):
        return r // (2 * nx), lax.rem(r // 2, nx), lax.rem(r, 2)

    def device(to_y, to_x, to_core):
        return z * 2 + to_core, lax.rem(to_y, tpn), (to_y // tpn) * nx + to_x

    def host(r):
        dl, dx, dc = split(r)
        h = lax.rem(core + dc, 2)
        to_x = lax.rem(xi + dx, nx)
        expert = lax.rem(tp + dl, tpn) * cpn + h * nx + to_x
        return expert, device(lax.rem(y + shift(dl, h) + yn, yn), to_x, h)

    def home(r):
        dl, dx, dc = split(r)
        return device(
            lax.rem(y - shift(dl, core) + yn, yn), lax.rem(xi - dx + nx, nx), lax.rem(core - dc + 2, 2)
        )

    def remote(src, dst, send, recv, device):
        return pltpu.make_async_remote_copy(
            src_ref=src, dst_ref=dst, send_sem=send, recv_sem=recv,
            device_id=device, device_id_type=MESH,
        )

    def wait_bytes(ref, sem):
        pltpu.make_async_copy(ref, ref, sem).wait()

    barrier = pltpu.get_barrier_semaphore()

    def greet(to):
        pl.semaphore_signal(barrier, inc=1, device_id=to, device_id_type=MESH)

    def greet_plane(r, carry):
        dy, rest = r // (2 * nx), lax.rem(r, 2 * nx)
        greet(device(lax.rem(y + dy, yn), lax.rem(xi + rest // 2, nx), lax.rem(core + rest, 2)))
        return carry

    def greet_dp(o, carry):
        greet((lax.rem(z + o // 2, nz) * 2 + lax.rem(o, 2), tp, cp))
        return carry

    lax.fori_loop(1, 2 * groups, greet_plane, 0)
    lax.fori_loop(2, dpn, greet_dp, 0)

    shards = [wg_ref[0], wu_ref[0], wd_ref[0]]
    for i in range(3):
        ws[i] = shards[i]

    @pl.when(core == yh)
    def _():
        for i in range(3):
            w[i, dp] = shards[i]

    tokens = tok_ref[...]
    grads = g_ref[...]
    expert = iota((LANES, t_count), 0)
    hot_t = [(expert == ids_ref[k : k + 1, :]).astype(F32) for k in range(2)]
    both_t = (hot_t[0] + hot_t[1]).astype(BF16)
    upper = (iota((t_count, t_count), 0) < iota((t_count, t_count), 1)).astype(BF16)
    before_t = mm(both_t, upper).astype(BF16)
    span = groups * ROWS
    spread_t = (iota((span, LANES), 0) // ROWS == iota((span, LANES), 1)).astype(BF16)
    slot_t = mm(spread_t, before_t)
    named_t = mm(spread_t, both_t) > 0.5
    row_t = lax.rem(iota((span, t_count), 0), ROWS)

    def choice(named, slot, row, j):
        wanted = row if j is None else jnp.where(row >= CAP, 3 * (row - CAP) + j, -1)
        return (named & (slot == wanted.astype(F32))).astype(BF16)

    main_t = choice(named_t, slot_t, row_t, None)
    tail_t = [choice(named_t, slot_t, row_t, j) for j in range(3)]

    def pack_home(values, out):
        for j in range(3):
            piece = mm(main_t, values[:, q * j : q * (j + 1)]) + mm(tail_t[j], values[:, 3 * q :])
            out[:, :, q * j : q * (j + 1)] = piece.astype(BF16).reshape(groups, ROWS, q)

    pack_home(tokens, sx)

    pl.semaphore_wait(barrier, 2 * groups - 1 + dpn - 2)

    def far(i):
        return remote(
            ws.at[i], w.at[i, dp], s_far.at[i], r_own.at[i],
            (z * 2 + yh, tp, (1 - yh) * nx + xi),
        )

    def pair(i):
        return remote(
            ws.at[i], w.at[i, dp], s_pair.at[i], r_own.at[i], (z * 2 + 1 - core, tp, cp)
        )

    for i in range(3):
        far(i).start()

    @pl.when(core != yh)
    def _():
        for i in range(3):
            pair(i).start()

    steps = nz // 2

    def ring(sign, step, i):
        at = pl.ds(lax.rem(z - sign * step + nz, nz) * 2, 2)
        index = ((0 if sign > 0 else steps) + step) * 3 + i
        return remote(
            w.at[i, at], w.at[i, at], s_ring.at[index], r_ring.at[index],
            (lax.rem(z + sign + nz, nz) * 2 + core, tp, cp),
        )

    links = {}
    for sign in (1, -1):
        for s in range(steps):
            for i in range(3):
                if s + 1 < steps or (i == 1) == (sign < 0):
                    links[sign, s, i] = ring(sign, s, i)

    def enter_ring():
        for i in range(3):
            for sign in (1, -1):
                if (sign, 0, i) in links:
                    links[sign, 0, i].start()

    def ring_step(s, chunks=(0, 1, 2)):
        for i in chunks:
            for sign in (1, -1):
                if (sign, s, i) in links:
                    links[sign, s, i].wait_recv()
                if (sign, s + 1, i) in links:
                    links[sign, s + 1, i].start()

    def send_in(src, dst, phase):
        for h in range(2):
            def one(r, carry):
                expert, to = host(r)
                remote(
                    src.at[expert], dst.at[r], s_in.at[2 * phase + h], r_in.at[2 * phase + h], to
                ).start()
                return carry

            lax.fori_loop(max(1, half * h), half * (h + 1), one, 0)

    send_in(sx, rx, 0)

    @pl.when(core == yh)
    def _():
        for i in range(3):
            wait_bytes(w.at[i, pl.ds(0, 1)], r_own.at[i])
        enter_ring()

    pack_home(grads, sg)
    send_in(sg, rg, 1)
    rx[0] = sx[mine]
    rg[0] = sg[mine]

    @pl.when(core != yh)
    def _():
        for i in range(3):
            wait_bytes(w.at[i, pl.ds(0, 2)], r_own.at[i])
        enter_ring()

    logits = mm_t(tokens, rw_ref[...])
    ecount = rw_ref.shape[0]
    hot = [hot_t[k].T for k in range(2)]
    both = hot[0] + hot[1]
    chosen = [jnp.sum(logits * hot[k][:, :ecount], axis=1, keepdims=True) for k in range(2)]
    mixing = [
        1.0 / (1.0 + jnp.exp(chosen[1] - chosen[0])),
        1.0 / (1.0 + jnp.exp(chosen[0] - chosen[1])),
    ]
    if steps > 1:
        ring_step(0)
    lower = (iota((t_count, t_count), 1) < iota((t_count, t_count), 0)).astype(BF16)
    before = mm(lower, both.astype(BF16)).astype(BF16)
    spread = (iota((LANES, span), 1) // ROWS == iota((LANES, span), 0)).astype(BF16)
    slot = mm(before, spread)
    row = lax.rem(iota((t_count, span), 1), ROWS)
    picks = []
    for k in range(2):
        named = mm(hot[k].astype(BF16), spread) > 0.5
        picks.append([choice(named, slot, row, None)] + [choice(named, slot, row, j) for j in range(3)])
    for s in range(1, steps - 1):
        ring_step(s)

    size = half * ROWS
    pr, qr = iota((size, size), 0), iota((size, size), 1)
    same = pr // ROWS == qr // ROWS
    pr, qr = lax.rem(pr, ROWS), lax.rem(qr, ROWS)
    unpack = [
        (same & (pr < CAP) & (qr >= CAP) & (pr == 3 * (qr - CAP) + j)).astype(BF16) for j in range(3)
    ]
    repack = [
        (same & (qr < CAP) & (pr >= CAP) & (qr == 3 * (pr - CAP) + j)).astype(BF16) for j in range(3)
    ]
    is_main = lax.rem(iota((size, q), 0), ROWS) < CAP

    def open_rows(ref, h):
        packed = ref[half * h : half * (h + 1)].reshape(size, 3 * q)
        tail = sum(mm(unpack[j], packed[:, q * j : q * (j + 1)]) for j in range(3))
        return jnp.concatenate([packed, tail.astype(BF16)], axis=1)

    def close_rows(values, ref, h):
        for j in range(3):
            piece = jnp.where(
                is_main, values[:, q * j : q * (j + 1)].astype(F32), mm(repack[j], values[:, 3 * q :])
            )
            ref[half * h : half * (h + 1), :, q * j : q * (j + 1)] = piece.astype(BF16).reshape(
                half, ROWS, q
            )

    def weight(i):
        return w[i].reshape(d, w.shape[3])

    def wait_in(ref, phase, h):
        lo = max(1, half * h)
        wait_bytes(ref.at[pl.ds(lo, half * (h + 1) - lo)], r_in.at[2 * phase + h])

    def send_out(src, dst, phase, h):
        def one(r, carry):
            remote(
                src.at[r], dst.at[mine], s_out.at[2 * phase + h], r_out.at[phase], home(r)
            ).start()
            return carry

        lax.fori_loop(max(1, half * h), half * (h + 1), one, 0)

    for h in range(2):
        wait_in(rx, 0, h)
        xs[size * h : size * (h + 1)] = open_rows(rx, h)
    for h in range(2):
        wait_in(rg, 1, h)
        gs[size * h : size * (h + 1)] = open_rows(rg, h)
    ring_step(steps - 1, (0, 1))
    for h in range(2):
        at = slice(size * h, size * (h + 1))
        act[at] = mm(xs[at], weight(0))
        up[at] = mm(xs[at], weight(1))
    ring_step(steps - 1, (2,))
    for h in range(2):
        at = slice(size * h, size * (h + 1))
        gate = act[at]
        hidden = (gate * jax.nn.sigmoid(gate) * up[at]).astype(BF16)
        close_rows(mm_t(hidden, weight(2)).astype(BF16), px, h)
        send_out(px, cx, 0, h)
    cx[mine] = px[0]
    for h in range(2):
        at = slice(size * h, size * (h + 1))
        grad_hidden = mm(gs[at], weight(2))
        gate = act[at]
        upper_act = up[at]
        sigma = jax.nn.sigmoid(gate)
        grad_gate = (grad_hidden * upper_act * sigma * (1.0 + gate * (1.0 - sigma))).astype(BF16)
        grad_up = (grad_hidden * gate * sigma).astype(BF16)
        back = mm_t(grad_gate, weight(0)) + mm_t(grad_up, weight(1))
        close_rows(back.astype(BF16), pg, h)
        send_out(pg, cg, 1, h)
    cg[mine] = pg[0]

    def home_rows(ref, k):
        packed = ref[...].reshape(span, 3 * q)
        main = mm(picks[k][0], packed)
        tail = sum(mm(picks[k][1 + j], packed[:, q * j : q * (j + 1)]) for j in range(3))
        return jnp.concatenate([main, tail], axis=1)

    wait_bytes(cx.at[pl.ds(0, groups - 1)], r_out.at[0])
    grads32 = grads.astype(F32)
    total = None
    scores = []
    for k in range(2):
        rows = home_rows(cx, k)
        scores.append(jnp.sum(grads32 * rows, axis=1, keepdims=True))
        total = mixing[k] * rows if total is None else total + mixing[k] * rows
    moe_ref[...] = total.astype(BF16)
    mean = mixing[0] * scores[0] + mixing[1] * scores[1]
    dense = sum(hot[k] * (mixing[k] * (scores[k] - mean)) for k in range(2))
    dense_t = dense.T.astype(BF16)
    part[...] = mm(dense_t, tokens)[: part.shape[0]]

    cw = r1.shape[2]
    nb = d // cw

    def chunk(c):
        return pl.ds(pl.multiple_of(8 * (c // nb), 8), 8), pl.ds(
            pl.multiple_of(cw * lax.rem(c, nb), LANES), cw
        )

    def scatter(o, carry):
        to = lax.rem(dp + o, dpn)
        remote(part.at[chunk(to)], r1.at[o - 1], s_ar.at[0], r_ar.at[0], (to, tp, cp)).start()
        return carry

    lax.fori_loop(1, dpn, scatter, 0)

    router_back = mm(dense.astype(BF16)[:, :ecount], rw_ref[...])

    wait_bytes(r1, r_ar.at[0])
    rows_own, cols_own = chunk(dp)
    ax[xi] = jnp.sum(r1[...], axis=0) + part[rows_own, cols_own]
    for o in range(1, nx):
        remote(
            ax.at[xi], ax.at[xi], s_ar.at[1], r_ar.at[1],
            (dp, tp, yh * nx + lax.rem(xi + o, nx)),
        ).start()
    wait_bytes(ax.at[pl.ds(0, nx - 1)], r_ar.at[1])
    ay[y] = jnp.sum(ax[...], axis=0)
    for o in range(1, yn):
        to = lax.rem(y + o, yn)
        remote(
            ay.at[y], ay.at[y], s_ar.at[2], r_ar.at[2],
            (dp, lax.rem(to, tpn), (to // tpn) * nx + xi),
        ).start()
    wait_bytes(ay.at[pl.ds(0, yn - 1)], r_ar.at[2])
    fin[dp] = jnp.sum(ay[...], axis=0)

    def gather(o, carry):
        to = lax.rem(dp + o, dpn)
        remote(fin.at[dp], fin.at[dp], s_ar.at[3], r_ar.at[3], (to, tp, cp)).start()
        return carry

    lax.fori_loop(1, dpn, gather, 0)

    wait_bytes(cg.at[pl.ds(0, groups - 1)], r_out.at[1])
    gt_ref[...] = (
        mixing[0] * home_rows(cg, 0) + mixing[1] * home_rows(cg, 1) + router_back
    ).astype(BF16)

    wait_bytes(fin.at[pl.ds(0, dpn - 1)], r_ar.at[3])
    for c in range(dpn):
        rg_ref[8 * (c // nb) : 8 * (c // nb) + 8, cw * (c % nb) : cw * (c % nb + 1)] = fin[c]

    for phase, ref in enumerate((sx, sg)):
        for h in range(2):
            lo = max(1, half * h)
            wait_bytes(ref.at[pl.ds(lo, half * (h + 1) - lo)], s_in.at[2 * phase + h])
    for phase, ref in enumerate((px, pg)):
        for h in range(2):
            lo = max(1, half * h)
            wait_bytes(ref.at[pl.ds(lo, half * (h + 1) - lo)], s_out.at[2 * phase + h])
    for i in range(3):
        far(i).wait_send()

    @pl.when(core != yh)
    def _():
        for i in range(3):
            pair(i).wait_send()

    for copy in links.values():
        copy.wait_send()
    wait_bytes(r1, s_ar.at[0])
    wait_bytes(ax.at[pl.ds(0, nx - 1)], s_ar.at[1])
    wait_bytes(ay.at[pl.ds(0, yn - 1)], s_ar.at[2])
    wait_bytes(fin.at[pl.ds(0, dpn - 1)], s_ar.at[3])


def on_device(tokens, expert_ids, router_weight, gate_weight, up_weight, down_weight, grad_out):
    sizes = tuple(lax.axis_size(name) for name in ("dp", "tp", "cp"))
    dpn, tpn, cpn = sizes
    groups = tpn * cpn
    t_count, d = tokens.shape
    shard, ff = gate_weight.shape[1:]
    block = pltpu.VMEM((groups, ROWS, 3 * d // 4), BF16)
    wide = 4 * d // dpn
    vmem = pl.BlockSpec(memory_space=pltpu.VMEM)
    dma = pltpu.SemaphoreType.DMA
    nz = dpn // 2
    moe, grad_tokens, router = pl.pallas_call(
        functools.partial(kernel, sizes),
        out_shape=(
            jax.ShapeDtypeStruct((t_count, d), BF16),
            jax.ShapeDtypeStruct((t_count, d), BF16),
            jax.ShapeDtypeStruct((32, d), F32),
        ),
        in_specs=[vmem] * 7,
        out_specs=(vmem,) * 3,
        scratch_shapes=[block] * 8
        + [
            pltpu.VMEM((groups * ROWS, d), BF16),
            pltpu.VMEM((groups * ROWS, d), BF16),
            pltpu.VMEM((groups * ROWS, ff), F32),
            pltpu.VMEM((groups * ROWS, ff), F32),
            pltpu.VMEM((3, shard, ff), BF16),
            pltpu.VMEM((3, dpn, shard, ff), BF16),
            pltpu.VMEM((32, d), F32),
            pltpu.VMEM((dpn - 1, 8, wide), F32),
            pltpu.VMEM((cpn // 2, 8, wide), F32),
            pltpu.VMEM((2 * tpn, 8, wide), F32),
            pltpu.VMEM((dpn, 8, wide), F32),
            dma((4,)), dma((4,)), dma((4,)), dma((2,)),
            dma((3 * nz,)), dma((3 * nz,)), dma((3,)), dma((3,)), dma((3,)),
            dma((4,)), dma((4,)),
        ],
        compiler_params=pltpu.CompilerParams(collective_id=0, has_side_effects=True),
        name="experts",
    )(
        tokens, expert_ids.T, router_weight.T, gate_weight, up_weight,
        jnp.swapaxes(down_weight, 1, 2), grad_out,
    )
    return moe, grad_tokens, router[: router_weight.shape[1]].T


def solution(mesh):
    in_specs = (
        P(("dp", "tp", "cp"), None),
        P(("dp", "tp", "cp"), None),
        P(),
        P(("tp", "cp"), "dp", None),
        P(("tp", "cp"), "dp", None),
        P(("tp", "cp"), None, "dp"),
        P(("dp", "tp", "cp"), None),
    )
    out_specs = (P(("dp", "tp", "cp"), None), P(("dp", "tp", "cp"), None), P())
    return jax.shard_map(
        on_device, mesh=mesh, in_specs=in_specs, out_specs=out_specs, check_vma=False
    )
```

```python
import functools

import jax
import jax.numpy as jnp
from jax import lax
from jax.experimental import pallas as pl
from jax.experimental.pallas import tpu as pltpu
from jax.sharding import PartitionSpec as P

MESH = pl.DeviceIdType.MESH
F32 = jnp.float32
BF16 = jnp.bfloat16
ROWS = 16
CAP = 12
LANES = 128


def iota(shape, dim):
    return lax.broadcasted_iota(jnp.int32, shape, dim)


def mm(a, b):
    return lax.dot_general(a, b, (((1,), (0,)), ((), ())), preferred_element_type=F32)


def mm_t(a, b):
    return lax.dot_general(a, b, (((1,), (1,)), ((), ())), preferred_element_type=F32)


def kernel(
    sizes,
    tok_ref, ids_ref, rw_ref, wg_ref, wu_ref, wd_ref, g_ref,
    moe_ref, gt_ref, rg_ref,
    sx, sg, rx, rg, px, pg, cx, cg, xs, gs, act, up, gh, so, si, ws, w, part, r1, ax, ay, fin,
    s_in, r_in, s_out, r_out, s_ring, r_ring, s_far, s_pair, r_own, s_ar, r_ar,
):
    dpn, tpn, cpn = sizes
    groups = tpn * cpn
    half = groups // 2
    nx = cpn // 2
    nz = dpn // 2
    t_count, d = tok_ref.shape
    q = d // 4
    dp = lax.axis_index("dp")
    tp = lax.axis_index("tp")
    cp = lax.axis_index("cp")
    xi = lax.rem(cp, nx)
    yh = cp // nx
    yn = 2 * tpn
    y = yh * tpn + tp
    z = dp // 2
    core = lax.rem(dp, 2)
    mine = tp * cpn + core * nx + xi

    def shift(dl, h):
        return dl - tpn * ((2 * dl + h) // (tpn + 1))

    xs_up = [lax.rem(xi + dx, nx) for dx in range(nx)]
    xs_down = [lax.rem(xi - dx + nx, nx) for dx in range(nx)]
    cores = [core, 1 - core]

    def column(to_y):
        return lax.rem(to_y, tpn), (to_y // tpn) * nx

    def each_host(h, fn):
        def run(dl, carry):
            to = [column(lax.rem(y + shift(dl, c) + yn, yn)) for c in range(2)]
            first = [
                (core * to[1 - dc][0] + (1 - core) * to[dc][0], core * to[1 - dc][1] + (1 - core) * to[dc][1])
                for dc in range(2)
            ]
            for j in range(2 * nx):
                dx, dc = j // 2, j % 2
                to_tp, base = first[dc]

                def send():
                    expert = to_tp * cpn + cores[dc] * nx + xs_up[dx]
                    fn(dl * (2 * nx) + j, expert, (z * 2 + cores[dc], to_tp, base + xs_up[dx]))

                if j:
                    send()
                else:
                    pl.when(dl > 0)(send)
            return carry

        lax.fori_loop(tpn // 2 * h, tpn // 2 * (h + 1), run, 0)

    def each_home(h, fn):
        def run(dl, carry):
            to_tp, base = column(lax.rem(y - shift(dl, core) + yn, yn))
            for j in range(2 * nx):
                dx, dc = j // 2, j % 2

                def send():
                    fn(dl * (2 * nx) + j, (z * 2 + cores[dc], to_tp, base + xs_down[dx]))

                if j:
                    send()
                else:
                    pl.when(dl > 0)(send)
            return carry

        lax.fori_loop(tpn // 2 * h, tpn // 2 * (h + 1), run, 0)

    def remote(src, dst, send, recv, device):
        return pltpu.make_async_remote_copy(
            src_ref=src, dst_ref=dst, send_sem=send, recv_sem=recv,
            device_id=device, device_id_type=MESH,
        )

    def wait_bytes(ref, sem):
        pltpu.make_async_copy(ref, ref, sem).wait()

    barrier = pltpu.get_barrier_semaphore()

    def greet(to):
        pl.semaphore_signal(barrier, inc=1, device_id=to, device_id_type=MESH)

    def greet_plane(to_tp, carry):
        for to_cp in range(cpn):
            for c in range(2):
                other = (to_tp != tp) | (cp != to_cp) | (core != c)
                pl.when(other)(functools.partial(greet, (z * 2 + c, to_tp, to_cp)))
        return carry

    lax.fori_loop(0, tpn, greet_plane, 0)
    for to in range(dpn):
        pl.when(z != to // 2)(functools.partial(greet, (to, tp, cp)))

    shards = [wg_ref[0], wu_ref[0], wd_ref[0]]
    for i in range(3):
        ws[i] = shards[i]

    @pl.when(core == yh)
    def _():
        for i in range(3):
            w[i, dp] = shards[i]

    tokens = tok_ref[...]
    grads = g_ref[...]
    expert = iota((LANES, t_count), 0)
    hot_t = [(expert == ids_ref[k : k + 1, :]).astype(F32) for k in range(2)]
    both_t = (hot_t[0] + hot_t[1]).astype(BF16)
    upper = (iota((t_count, t_count), 0) < iota((t_count, t_count), 1)).astype(BF16)
    before_t = mm(both_t, upper).astype(BF16)
    span = groups * ROWS
    spread_t = (iota((span, LANES), 0) // ROWS == iota((span, LANES), 1)).astype(BF16)
    slot_t = mm(spread_t, before_t)
    named_t = mm(spread_t, both_t) > 0.5
    row_t = lax.rem(iota((span, t_count), 0), ROWS)

    def choice(named, slot, row, j):
        wanted = row if j is None else jnp.where(row >= CAP, 3 * (row - CAP) + j, -1)
        return (named & (slot == wanted.astype(F32))).astype(BF16)

    main_t = choice(named_t, slot_t, row_t, None)
    tail_t = [choice(named_t, slot_t, row_t, j) for j in range(3)]

    def pack_home(values, out):
        for j in range(3):
            piece = mm(main_t, values[:, q * j : q * (j + 1)]) + mm(tail_t[j], values[:, 3 * q :])
            out[:, :, q * j : q * (j + 1)] = piece.astype(BF16).reshape(groups, ROWS, q)

    pack_home(tokens, sx)

    pl.semaphore_wait(barrier, 2 * groups - 1 + dpn - 2)

    def far(i):
        return remote(
            ws.at[i], w.at[i, dp], s_far.at[i], r_own.at[i],
            (z * 2 + yh, tp, (1 - yh) * nx + xi),
        )

    def pair(i):
        return remote(
            ws.at[i], w.at[i, dp], s_pair.at[i], r_own.at[i], (z * 2 + 1 - core, tp, cp)
        )

    for i in range(3):
        far(i).start()

    @pl.when(core != yh)
    def _():
        for i in range(3):
            pair(i).start()

    steps = nz // 2

    def ring(sign, step, i):
        at = pl.ds(lax.rem(z - sign * step + nz, nz) * 2, 2)
        index = ((0 if sign > 0 else steps) + step) * 3 + i
        return remote(
            w.at[i, at], w.at[i, at], s_ring.at[index], r_ring.at[index],
            (lax.rem(z + sign + nz, nz) * 2 + core, tp, cp),
        )

    links = {}
    for sign in (1, -1):
        for s in range(steps):
            for i in range(3):
                if s + 1 < steps or (i == 1) == (sign < 0):
                    links[sign, s, i] = ring(sign, s, i)

    def enter_ring():
        for i in range(3):
            for sign in (1, -1):
                if (sign, 0, i) in links:
                    links[sign, 0, i].start()

    def ring_step(s, chunks=(0, 1, 2)):
        for i in chunks:
            for sign in (1, -1):
                if (sign, s, i) in links:
                    links[sign, s, i].wait_recv()
                if (sign, s + 1, i) in links:
                    links[sign, s + 1, i].start()

    def send_in(src, dst, phase):
        for h in range(2):
            index = 2 * phase + h
            each_host(h, lambda r, expert, to: remote(
                src.at[expert], dst.at[r], s_in.at[index], r_in.at[index], to
            ).start())

    send_in(sx, rx, 0)

    @pl.when(core == yh)
    def _():
        for i in range(3):
            wait_bytes(w.at[i, pl.ds(0, 1)], r_own.at[i])
        enter_ring()

    pack_home(grads, sg)
    send_in(sg, rg, 1)
    rx[0] = sx[mine]
    rg[0] = sg[mine]

    @pl.when(core != yh)
    def _():
        for i in range(3):
            wait_bytes(w.at[i, pl.ds(0, 2)], r_own.at[i])
        enter_ring()

    logits = mm_t(tokens, rw_ref[...])
    ecount = rw_ref.shape[0]
    hot = [hot_t[k].T for k in range(2)]
    both = hot[0] + hot[1]
    chosen = [jnp.sum(logits * hot[k][:, :ecount], axis=1, keepdims=True) for k in range(2)]
    mixing = [
        1.0 / (1.0 + jnp.exp(chosen[1] - chosen[0])),
        1.0 / (1.0 + jnp.exp(chosen[0] - chosen[1])),
    ]
    if steps > 1:
        ring_step(0)
    lower = (iota((t_count, t_count), 1) < iota((t_count, t_count), 0)).astype(BF16)
    before = mm(lower, both.astype(BF16)).astype(BF16)
    spread = (iota((LANES, span), 1) // ROWS == iota((LANES, span), 0)).astype(BF16)
    slot = mm(before, spread)
    row = lax.rem(iota((t_count, span), 1), ROWS)
    slots = [jnp.sum(before.astype(F32) * hot[k], axis=1, keepdims=True) for k in range(2)]
    picks = []
    for k in range(2):
        named = mm(hot[k].astype(BF16), spread) > 0.5
        picks.append([choice(named, slot, row, None)] + [choice(named, slot, row, j) for j in range(3)])
    for s in range(1, steps - 1):
        ring_step(s)

    size = half * ROWS
    pr, qr = iota((size, size), 0), iota((size, size), 1)
    same = pr // ROWS == qr // ROWS
    pr, qr = lax.rem(pr, ROWS), lax.rem(qr, ROWS)
    unpack = [
        (same & (pr < CAP) & (qr >= CAP) & (pr == 3 * (qr - CAP) + j)).astype(BF16) for j in range(3)
    ]
    repack = [
        (same & (qr < CAP) & (pr >= CAP) & (qr == 3 * (pr - CAP) + j)).astype(BF16) for j in range(3)
    ]
    is_main = lax.rem(iota((size, q), 0), ROWS) < CAP

    def open_rows(ref, h):
        packed = ref[half * h : half * (h + 1)].reshape(size, 3 * q)
        tail = sum(mm(unpack[j], packed[:, q * j : q * (j + 1)]) for j in range(3))
        return jnp.concatenate([packed, tail.astype(BF16)], axis=1)

    def close_rows(values, ref, h):
        for j in range(3):
            piece = jnp.where(
                is_main, values[:, q * j : q * (j + 1)].astype(F32), mm(repack[j], values[:, 3 * q :])
            )
            ref[half * h : half * (h + 1), :, q * j : q * (j + 1)] = piece.astype(BF16).reshape(
                half, ROWS, q
            )

    def weight(i):
        return w[i].reshape(d, w.shape[3])

    def wait_in(ref, phase, h):
        lo = max(1, half * h)
        wait_bytes(ref.at[pl.ds(lo, half * (h + 1) - lo)], r_in.at[2 * phase + h])

    def send_out(src, dst, phase, h):
        index = 2 * phase + h
        each_home(h, lambda r, to: remote(
            src.at[r], dst.at[mine], s_out.at[index], r_out.at[phase], to
        ).start())

    for h in range(2):
        wait_in(rx, 0, h)
        xs[size * h : size * (h + 1)] = open_rows(rx, h)
    for h in range(2):
        wait_in(rg, 1, h)
        gs[size * h : size * (h + 1)] = open_rows(rg, h)
    ring_step(steps - 1, (0, 1))
    for h in range(2):
        at = slice(size * h, size * (h + 1))
        act[at] = mm(xs[at], weight(0))
        up[at] = mm(xs[at], weight(1))
    ring_step(steps - 1, (2,))
    hiddens = []
    lanes = iota((size, LANES), 1)
    own_lane = lanes == lax.rem(iota((size, LANES), 0), ROWS)
    for h in range(2):
        at = slice(size * h, size * (h + 1))
        gate = act[at]
        hidden = (gate * jax.nn.sigmoid(gate) * up[at]).astype(BF16)
        hiddens.append(hidden)
        grad_hidden = mm(gs[at], weight(2))
        gh[at] = grad_hidden
        score = jnp.sum(hidden.astype(F32) * grad_hidden, axis=1, keepdims=True)
        table = jnp.where(own_lane, score, 0.0).reshape(half, ROWS, LANES)
        so[half * h : half * (h + 1)] = jnp.sum(table, axis=1, keepdims=True)
    for h in range(2):
        each_home(h, lambda r, to: remote(so.at[r], si.at[mine], s_ar.at[4], r_ar.at[4], to).start())
    si[mine] = so[0]
    for h in range(2):
        close_rows(mm_t(hiddens[h], weight(2)).astype(BF16), px, h)
        send_out(px, cx, 0, h)
    cx[mine] = px[0]
    for h in range(2):
        at = slice(size * h, size * (h + 1))
        grad_hidden, gate, upper_act = gh[at], act[at], up[at]
        sigma = jax.nn.sigmoid(gate)
        grad_gate = (grad_hidden * upper_act * sigma * (1.0 + gate * (1.0 - sigma))).astype(BF16)
        grad_up = (grad_hidden * gate * sigma).astype(BF16)
        back = mm_t(grad_gate, weight(0)) + mm_t(grad_up, weight(1))
        close_rows(back.astype(BF16), pg, h)
    cg[mine] = pg[0]

    def home_rows(ref, k):
        packed = ref[...].reshape(span, 3 * q)
        main = mm(picks[k][0], packed)
        tail = sum(mm(picks[k][1 + j], packed[:, q * j : q * (j + 1)]) for j in range(3))
        return jnp.concatenate([main, tail], axis=1)

    wait_bytes(si.at[pl.ds(0, groups - 1)], r_ar.at[4])
    rest = si[...].reshape(groups, LANES)
    pieces = []
    for _ in range(3):
        pieces.append(rest.astype(BF16))
        rest = rest - pieces[-1].astype(F32)
    token_lane = iota((t_count, LANES), 1).astype(F32)
    scores = []
    for k in range(2):
        of_expert = hot[k][:, :groups].astype(BF16)
        found = sum(mm(of_expert, piece) for piece in pieces)
        scores.append(
            jnp.sum(jnp.where(token_lane == slots[k], found, 0.0), axis=1, keepdims=True)
        )
    mean = mixing[0] * scores[0] + mixing[1] * scores[1]
    dense = sum(hot[k] * (mixing[k] * (scores[k] - mean)) for k in range(2))
    dense_t = dense.T.astype(BF16)
    part[...] = mm(dense_t, tokens)[: part.shape[0]]

    cw = r1.shape[2]
    nb = d // cw

    def chunk(c):
        return slice(8 * (c // nb), 8 * (c // nb) + 8), slice(cw * (c % nb), cw * (c % nb + 1))

    for to in range(dpn):
        rows_to, cols_to = chunk(to)

        @pl.when(dp != to)
        def _():
            remote(
                part.at[rows_to, cols_to], r1.at[dp], s_ar.at[0], r_ar.at[0], (to, tp, cp)
            ).start()

        @pl.when(dp == to)
        def _():
            r1[dp] = part[rows_to, cols_to]

    router_back = mm(dense.astype(BF16)[:, :ecount], rw_ref[...])

    wait_bytes(r1.at[pl.ds(0, dpn - 1)], r_ar.at[0])
    ax[xi] = jnp.sum(r1[...], axis=0)
    for o in range(1, nx):
        remote(
            ax.at[xi], ax.at[xi], s_ar.at[1], r_ar.at[1], (dp, tp, yh * nx + xs_up[o])
        ).start()
    send_out(pg, cg, 1, 0)
    wait_bytes(ax.at[pl.ds(0, nx - 1)], r_ar.at[1])
    ay[y] = jnp.sum(ax[...], axis=0)
    for o in range(1, yn):
        to_tp, base = column(lax.rem(y + o, yn))
        remote(ay.at[y], ay.at[y], s_ar.at[2], r_ar.at[2], (dp, to_tp, base + xi)).start()
    send_out(pg, cg, 1, 1)

    wait_bytes(cx.at[pl.ds(0, groups - 1)], r_out.at[0])
    moe_ref[...] = (mixing[0] * home_rows(cx, 0) + mixing[1] * home_rows(cx, 1)).astype(BF16)

    wait_bytes(ay.at[pl.ds(0, yn - 1)], r_ar.at[2])
    fin[dp] = jnp.sum(ay[...], axis=0)
    for to in range(dpn):
        @pl.when(dp != to)
        def _():
            remote(fin.at[dp], fin.at[dp], s_ar.at[3], r_ar.at[3], (to, tp, cp)).start()

    wait_bytes(cg.at[pl.ds(0, groups - 1)], r_out.at[1])
    gt_ref[...] = (
        mixing[0] * home_rows(cg, 0) + mixing[1] * home_rows(cg, 1) + router_back
    ).astype(BF16)

    wait_bytes(fin.at[pl.ds(0, dpn - 1)], r_ar.at[3])
    for c in range(dpn):
        rg_ref[chunk(c)] = fin[c]

    for phase, ref in enumerate((sx, sg)):
        for h in range(2):
            lo = max(1, half * h)
            wait_bytes(ref.at[pl.ds(lo, half * (h + 1) - lo)], s_in.at[2 * phase + h])
    for phase, ref in enumerate((px, pg)):
        for h in range(2):
            lo = max(1, half * h)
            wait_bytes(ref.at[pl.ds(lo, half * (h + 1) - lo)], s_out.at[2 * phase + h])
    for i in range(3):
        far(i).wait_send()

    @pl.when(core != yh)
    def _():
        for i in range(3):
            pair(i).wait_send()

    for copy in links.values():
        copy.wait_send()
    wait_bytes(r1.at[pl.ds(0, dpn - 1)], s_ar.at[0])
    wait_bytes(so.at[pl.ds(0, groups - 1)], s_ar.at[4])
    wait_bytes(ax.at[pl.ds(0, nx - 1)], s_ar.at[1])
    wait_bytes(ay.at[pl.ds(0, yn - 1)], s_ar.at[2])
    wait_bytes(fin.at[pl.ds(0, dpn - 1)], s_ar.at[3])


def on_device(tokens, expert_ids, router_weight, gate_weight, up_weight, down_weight, grad_out):
    sizes = tuple(lax.axis_size(name) for name in ("dp", "tp", "cp"))
    dpn, tpn, cpn = sizes
    groups = tpn * cpn
    t_count, d = tokens.shape
    shard, ff = gate_weight.shape[1:]
    block = pltpu.VMEM((groups, ROWS, 3 * d // 4), BF16)
    wide = 4 * d // dpn
    vmem = pl.BlockSpec(memory_space=pltpu.VMEM)
    dma = pltpu.SemaphoreType.DMA
    nz = dpn // 2
    moe, grad_tokens, router = pl.pallas_call(
        functools.partial(kernel, sizes),
        out_shape=(
            jax.ShapeDtypeStruct((t_count, d), BF16),
            jax.ShapeDtypeStruct((t_count, d), BF16),
            jax.ShapeDtypeStruct((32, d), F32),
        ),
        in_specs=[vmem] * 7,
        out_specs=(vmem,) * 3,
        scratch_shapes=[block] * 8
        + [
            pltpu.VMEM((groups * ROWS, d), BF16),
            pltpu.VMEM((groups * ROWS, d), BF16),
            pltpu.VMEM((groups * ROWS, ff), F32),
            pltpu.VMEM((groups * ROWS, ff), F32),
            pltpu.VMEM((groups * ROWS, ff), F32),
            pltpu.VMEM((groups, 1, LANES), F32),
            pltpu.VMEM((groups, 1, LANES), F32),
            pltpu.VMEM((3, shard, ff), BF16),
            pltpu.VMEM((3, dpn, shard, ff), BF16),
            pltpu.VMEM((32, d), F32),
            pltpu.VMEM((dpn, 8, wide), F32),
            pltpu.VMEM((cpn // 2, 8, wide), F32),
            pltpu.VMEM((2 * tpn, 8, wide), F32),
            pltpu.VMEM((dpn, 8, wide), F32),
            dma((4,)), dma((4,)), dma((4,)), dma((2,)),
            dma((3 * nz,)), dma((3 * nz,)), dma((3,)), dma((3,)), dma((3,)),
            dma((5,)), dma((5,)),
        ],
        compiler_params=pltpu.CompilerParams(collective_id=0, has_side_effects=True),
        name="experts",
    )(
        tokens, expert_ids.T, router_weight.T, gate_weight, up_weight,
        jnp.swapaxes(down_weight, 1, 2), grad_out,
    )
    return moe, grad_tokens, router[: router_weight.shape[1]].T


def solution(mesh):
    in_specs = (
        P(("dp", "tp", "cp"), None),
        P(("dp", "tp", "cp"), None),
        P(),
        P(("tp", "cp"), "dp", None),
        P(("tp", "cp"), "dp", None),
        P(("tp", "cp"), None, "dp"),
        P(("dp", "tp", "cp"), None),
    )
    out_specs = (P(("dp", "tp", "cp"), None), P(("dp", "tp", "cp"), None), P())
    return jax.shard_map(
        on_device, mesh=mesh, in_specs=in_specs, out_specs=out_specs, check_vma=False
    )
```

```python
import functools

import jax
import jax.numpy as jnp
from jax import lax
from jax.experimental import pallas as pl
from jax.experimental.pallas import tpu as pltpu
from jax.sharding import PartitionSpec as P

MESH = pl.DeviceIdType.MESH
F32 = jnp.float32
BF16 = jnp.bfloat16
ROWS = 16
CAP = 12
LANES = 128


def iota(shape, dim):
    return lax.broadcasted_iota(jnp.int32, shape, dim)


def mm(a, b):
    return lax.dot_general(a, b, (((1,), (0,)), ((), ())), preferred_element_type=F32)


def mm_t(a, b):
    return lax.dot_general(a, b, (((1,), (1,)), ((), ())), preferred_element_type=F32)


def kernel(
    sizes,
    tok_ref, ids_ref, rw_ref, wg_ref, wu_ref, wd_ref, g_ref,
    moe_ref, gt_ref, rg_ref,
    sx, sg, rx, rg, px, pg, cx, cg, xs, gs, act, up, gh, so, si, ws, wr, w, part, r1, ax, ay, fin,
    s_in, r_in, s_out, r_out, s_ring, r_ring, s_far, s_mid, s_pair, r_mid, r_own, s_ar, r_ar,
):
    dpn, tpn, cpn = sizes
    groups = tpn * cpn
    half = groups // 2
    nx = cpn // 2
    nz = dpn // 2
    t_count, d = tok_ref.shape
    q = d // 4
    dp = lax.axis_index("dp")
    tp = lax.axis_index("tp")
    cp = lax.axis_index("cp")
    xi = lax.rem(cp, nx)
    yh = cp // nx
    yn = 2 * tpn
    y = yh * tpn + tp
    z = dp // 2
    core = lax.rem(dp, 2)
    mine = tp * cpn + core * nx + xi

    def shift(dl, h):
        return dl - tpn * ((2 * dl + h) // (tpn + 1))

    xs_up = [lax.rem(xi + dx, nx) for dx in range(nx)]
    xs_down = [lax.rem(xi - dx + nx, nx) for dx in range(nx)]
    cores = [core, 1 - core]

    def column(to_y):
        return lax.rem(to_y, tpn), (to_y // tpn) * nx

    def each_host(h, fn):
        def run(dl, carry):
            to = [column(lax.rem(y + shift(dl, c) + yn, yn)) for c in range(2)]
            first = [
                (core * to[1 - dc][0] + (1 - core) * to[dc][0], core * to[1 - dc][1] + (1 - core) * to[dc][1])
                for dc in range(2)
            ]
            for j in range(2 * nx):
                dx, dc = j // 2, j % 2
                to_tp, base = first[dc]

                def send():
                    expert = to_tp * cpn + cores[dc] * nx + xs_up[dx]
                    fn(dl * (2 * nx) + j, expert, (z * 2 + cores[dc], to_tp, base + xs_up[dx]))

                if j:
                    send()
                else:
                    pl.when(dl > 0)(send)
            return carry

        lax.fori_loop(tpn // 2 * h, tpn // 2 * (h + 1), run, 0)

    def each_home(h, fn):
        def run(dl, carry):
            to_tp, base = column(lax.rem(y - shift(dl, core) + yn, yn))
            for j in range(2 * nx):
                dx, dc = j // 2, j % 2

                def send():
                    fn(dl * (2 * nx) + j, (z * 2 + cores[dc], to_tp, base + xs_down[dx]))

                if j:
                    send()
                else:
                    pl.when(dl > 0)(send)
            return carry

        lax.fori_loop(tpn // 2 * h, tpn // 2 * (h + 1), run, 0)

    def remote(src, dst, send, recv, device):
        return pltpu.make_async_remote_copy(
            src_ref=src, dst_ref=dst, send_sem=send, recv_sem=recv,
            device_id=device, device_id_type=MESH,
        )

    def wait_bytes(ref, sem):
        pltpu.make_async_copy(ref, ref, sem).wait()

    barrier = pltpu.get_barrier_semaphore()

    def greet(to):
        pl.semaphore_signal(barrier, inc=1, device_id=to, device_id_type=MESH)

    def greet_plane(to_tp, carry):
        for to_cp in range(cpn):
            for c in range(2):
                other = (to_tp != tp) | (cp != to_cp) | (core != c)
                pl.when(other)(functools.partial(greet, (z * 2 + c, to_tp, to_cp)))
        return carry

    lax.fori_loop(0, tpn, greet_plane, 0)
    for to in range(dpn):
        pl.when(z != to // 2)(functools.partial(greet, (to, tp, cp)))

    shards = [wg_ref[0], wu_ref[0], wd_ref[0]]
    for i in range(3):
        ws[i] = shards[i]

    @pl.when(core == yh)
    def _():
        for i in range(3):
            w[i, dp] = shards[i]

    tokens = tok_ref[...]
    grads = g_ref[...]
    expert = iota((LANES, t_count), 0)
    hot_t = [(expert == ids_ref[k : k + 1, :]).astype(F32) for k in range(2)]
    both_t = (hot_t[0] + hot_t[1]).astype(BF16)
    upper = (iota((t_count, t_count), 0) < iota((t_count, t_count), 1)).astype(BF16)
    before_t = mm(both_t, upper).astype(BF16)
    span = groups * ROWS
    spread_t = (iota((span, LANES), 0) // ROWS == iota((span, LANES), 1)).astype(BF16)
    slot_t = mm(spread_t, before_t)
    named_t = mm(spread_t, both_t) > 0.5
    row_t = lax.rem(iota((span, t_count), 0), ROWS)

    def choice(named, slot, row, j):
        wanted = row if j is None else jnp.where(row >= CAP, 3 * (row - CAP) + j, -1)
        return (named & (slot == wanted.astype(F32))).astype(BF16)

    main_t = choice(named_t, slot_t, row_t, None)
    tail_t = [choice(named_t, slot_t, row_t, j) for j in range(3)]

    def pack_home(values, out):
        for j in range(3):
            piece = mm(main_t, values[:, q * j : q * (j + 1)]) + mm(tail_t[j], values[:, 3 * q :])
            out[:, :, q * j : q * (j + 1)] = piece.astype(BF16).reshape(groups, ROWS, q)

    pack_home(tokens, sx)

    pl.semaphore_wait(barrier, 2 * groups - 1 + dpn - 2)

    hop = (yn // 4) * (1 - 2 * core)
    hop_tp, hop_base = column(lax.rem(y + hop + yn, yn))
    from_yh = lax.rem(y - hop + yn, yn) // tpn

    def far(i):
        return remote(
            ws.at[i], wr.at[i], s_far.at[i], r_mid.at[i], (dp, hop_tp, hop_base + xi)
        )

    def relay(i):
        return remote(
            wr.at[i], w.at[i, dp], s_mid.at[i], r_own.at[i],
            (z * 2 + from_yh, hop_tp, hop_base + xi),
        )

    def pair(i):
        return remote(
            ws.at[i], w.at[i, dp], s_pair.at[i], r_own.at[i], (z * 2 + 1 - core, tp, cp)
        )

    for i in range(3):
        far(i).start()

    @pl.when(core != yh)
    def _():
        for i in range(3):
            pair(i).start()

    steps = nz // 2

    def ring(sign, step, i):
        at = pl.ds(lax.rem(z - sign * step + nz, nz) * 2, 2)
        index = ((0 if sign > 0 else steps) + step) * 3 + i
        return remote(
            w.at[i, at], w.at[i, at], s_ring.at[index], r_ring.at[index],
            (lax.rem(z + sign + nz, nz) * 2 + core, tp, cp),
        )

    links = {}
    for sign in (1, -1):
        for s in range(steps):
            for i in range(3):
                if s + 1 < steps or (i == 1) == (sign < 0):
                    links[sign, s, i] = ring(sign, s, i)

    def enter_ring():
        for i in range(3):
            for sign in (1, -1):
                if (sign, 0, i) in links:
                    links[sign, 0, i].start()

    def ring_step(s, chunks=(0, 1, 2)):
        for i in chunks:
            for sign in (1, -1):
                if (sign, s, i) in links:
                    links[sign, s, i].wait_recv()
                if (sign, s + 1, i) in links:
                    links[sign, s + 1, i].start()

    def send_in(src, dst, phase):
        for h in range(2):
            index = 2 * phase + h
            each_host(h, lambda r, expert, to: remote(
                src.at[expert], dst.at[r], s_in.at[index], r_in.at[index], to
            ).start())

    @pl.when(core == yh)
    def _():
        for i in range(3):
            wait_bytes(w.at[i, pl.ds(0, 1)], r_own.at[i])
        enter_ring()

    for i in range(3):
        far(i).wait_recv()
        relay(i).start()
    pack_home(grads, sg)

    @pl.when(core != yh)
    def _():
        for i in range(3):
            wait_bytes(w.at[i, pl.ds(0, 2)], r_own.at[i])
        enter_ring()

    send_in(sx, rx, 0)
    send_in(sg, rg, 1)
    rx[0] = sx[mine]
    rg[0] = sg[mine]

    logits = mm_t(tokens, rw_ref[...])
    ecount = rw_ref.shape[0]
    hot = [hot_t[k].T for k in range(2)]
    both = hot[0] + hot[1]
    chosen = [jnp.sum(logits * hot[k][:, :ecount], axis=1, keepdims=True) for k in range(2)]
    mixing = [
        1.0 / (1.0 + jnp.exp(chosen[1] - chosen[0])),
        1.0 / (1.0 + jnp.exp(chosen[0] - chosen[1])),
    ]
    if steps > 1:
        ring_step(0)
    lower = (iota((t_count, t_count), 1) < iota((t_count, t_count), 0)).astype(BF16)
    before = mm(lower, both.astype(BF16)).astype(BF16)
    spread = (iota((LANES, span), 1) // ROWS == iota((LANES, span), 0)).astype(BF16)
    slot = mm(before, spread)
    row = lax.rem(iota((t_count, span), 1), ROWS)
    slots = [jnp.sum(before.astype(F32) * hot[k], axis=1, keepdims=True) for k in range(2)]
    picks = []
    for k in range(2):
        named = mm(hot[k].astype(BF16), spread) > 0.5
        picks.append([choice(named, slot, row, None)] + [choice(named, slot, row, j) for j in range(3)])
    for s in range(1, steps - 1):
        ring_step(s)

    size = half * ROWS
    pr, qr = iota((size, size), 0), iota((size, size), 1)
    same = pr // ROWS == qr // ROWS
    pr, qr = lax.rem(pr, ROWS), lax.rem(qr, ROWS)
    unpack = [
        (same & (pr < CAP) & (qr >= CAP) & (pr == 3 * (qr - CAP) + j)).astype(BF16) for j in range(3)
    ]
    repack = [
        (same & (qr < CAP) & (pr >= CAP) & (qr == 3 * (pr - CAP) + j)).astype(BF16) for j in range(3)
    ]
    is_main = lax.rem(iota((size, q), 0), ROWS) < CAP

    def open_rows(ref, h):
        packed = ref[half * h : half * (h + 1)].reshape(size, 3 * q)
        tail = sum(mm(unpack[j], packed[:, q * j : q * (j + 1)]) for j in range(3))
        return jnp.concatenate([packed, tail.astype(BF16)], axis=1)

    def close_rows(values, ref, h):
        for j in range(3):
            piece = jnp.where(
                is_main, values[:, q * j : q * (j + 1)].astype(F32), mm(repack[j], values[:, 3 * q :])
            )
            ref[half * h : half * (h + 1), :, q * j : q * (j + 1)] = piece.astype(BF16).reshape(
                half, ROWS, q
            )

    def weight(i):
        return w[i].reshape(d, w.shape[3])

    def wait_in(ref, phase, h):
        lo = max(1, half * h)
        wait_bytes(ref.at[pl.ds(lo, half * (h + 1) - lo)], r_in.at[2 * phase + h])

    def send_out(src, dst, phase, h):
        index = 2 * phase + h
        each_home(h, lambda r, to: remote(
            src.at[r], dst.at[mine], s_out.at[index], r_out.at[phase], to
        ).start())

    for h in range(2):
        wait_in(rx, 0, h)
        xs[size * h : size * (h + 1)] = open_rows(rx, h)
    for h in range(2):
        wait_in(rg, 1, h)
        gs[size * h : size * (h + 1)] = open_rows(rg, h)
    ring_step(steps - 1, (0, 1))
    for h in range(2):
        at = slice(size * h, size * (h + 1))
        act[at] = mm(xs[at], weight(0))
        up[at] = mm(xs[at], weight(1))
    ring_step(steps - 1, (2,))
    hiddens = []
    lanes = iota((size, LANES), 1)
    own_lane = lanes == lax.rem(iota((size, LANES), 0), ROWS)
    for h in range(2):
        at = slice(size * h, size * (h + 1))
        gate = act[at]
        hidden = (gate * jax.nn.sigmoid(gate) * up[at]).astype(BF16)
        hiddens.append(hidden)
        grad_hidden = mm(gs[at], weight(2))
        gh[at] = grad_hidden
        score = jnp.sum(hidden.astype(F32) * grad_hidden, axis=1, keepdims=True)
        table = jnp.where(own_lane, score, 0.0).reshape(half, ROWS, LANES)
        so[half * h : half * (h + 1)] = jnp.sum(table, axis=1, keepdims=True)
    for h in range(2):
        each_home(h, lambda r, to: remote(so.at[r], si.at[mine], s_ar.at[4], r_ar.at[4], to).start())
    si[mine] = so[0]
    for h in range(2):
        close_rows(mm_t(hiddens[h], weight(2)).astype(BF16), px, h)
        send_out(px, cx, 0, h)
    cx[mine] = px[0]
    for h in range(2):
        at = slice(size * h, size * (h + 1))
        grad_hidden, gate, upper_act = gh[at], act[at], up[at]
        sigma = jax.nn.sigmoid(gate)
        grad_gate = (grad_hidden * upper_act * sigma * (1.0 + gate * (1.0 - sigma))).astype(BF16)
        grad_up = (grad_hidden * gate * sigma).astype(BF16)
        back = mm_t(grad_gate, weight(0)) + mm_t(grad_up, weight(1))
        close_rows(back.astype(BF16), pg, h)
    cg[mine] = pg[0]

    def home_rows(ref, k):
        packed = ref[...].reshape(span, 3 * q)
        main = mm(picks[k][0], packed)
        tail = sum(mm(picks[k][1 + j], packed[:, q * j : q * (j + 1)]) for j in range(3))
        return jnp.concatenate([main, tail], axis=1)

    wait_bytes(si.at[pl.ds(0, groups - 1)], r_ar.at[4])
    rest = si[...].reshape(groups, LANES)
    pieces = []
    for _ in range(3):
        pieces.append(rest.astype(BF16))
        rest = rest - pieces[-1].astype(F32)
    token_lane = iota((t_count, LANES), 1).astype(F32)
    scores = []
    for k in range(2):
        of_expert = hot[k][:, :groups].astype(BF16)
        found = sum(mm(of_expert, piece) for piece in pieces)
        scores.append(
            jnp.sum(jnp.where(token_lane == slots[k], found, 0.0), axis=1, keepdims=True)
        )
    mean = mixing[0] * scores[0] + mixing[1] * scores[1]
    dense = sum(hot[k] * (mixing[k] * (scores[k] - mean)) for k in range(2))
    dense_t = dense.T.astype(BF16)
    part[...] = mm(dense_t, tokens)[: part.shape[0]]

    cw = r1.shape[2]
    nb = d // cw

    def chunk(c):
        return slice(8 * (c // nb), 8 * (c // nb) + 8), slice(cw * (c % nb), cw * (c % nb + 1))

    for to in range(dpn):
        rows_to, cols_to = chunk(to)

        @pl.when(dp != to)
        def _():
            remote(
                part.at[rows_to, cols_to], r1.at[dp], s_ar.at[0], r_ar.at[0], (to, tp, cp)
            ).start()

        @pl.when(dp == to)
        def _():
            r1[dp] = part[rows_to, cols_to]

    router_back = mm(dense.astype(BF16)[:, :ecount], rw_ref[...])

    wait_bytes(r1.at[pl.ds(0, dpn - 1)], r_ar.at[0])
    ax[xi] = jnp.sum(r1[...], axis=0)
    for o in range(1, nx):
        remote(
            ax.at[xi], ax.at[xi], s_ar.at[1], r_ar.at[1], (dp, tp, yh * nx + xs_up[o])
        ).start()
    send_out(pg, cg, 1, 0)
    wait_bytes(ax.at[pl.ds(0, nx - 1)], r_ar.at[1])
    ay[y] = jnp.sum(ax[...], axis=0)
    for o in range(1, yn):
        to_tp, base = column(lax.rem(y + o, yn))
        remote(ay.at[y], ay.at[y], s_ar.at[2], r_ar.at[2], (dp, to_tp, base + xi)).start()
    send_out(pg, cg, 1, 1)

    wait_bytes(cx.at[pl.ds(0, groups - 1)], r_out.at[0])
    moe_ref[...] = (mixing[0] * home_rows(cx, 0) + mixing[1] * home_rows(cx, 1)).astype(BF16)

    wait_bytes(ay.at[pl.ds(0, yn - 1)], r_ar.at[2])
    fin[dp] = jnp.sum(ay[...], axis=0)
    for to in range(dpn):
        @pl.when(dp != to)
        def _():
            remote(fin.at[dp], fin.at[dp], s_ar.at[3], r_ar.at[3], (to, tp, cp)).start()

    wait_bytes(cg.at[pl.ds(0, groups - 1)], r_out.at[1])
    gt_ref[...] = (
        mixing[0] * home_rows(cg, 0) + mixing[1] * home_rows(cg, 1) + router_back
    ).astype(BF16)

    wait_bytes(fin.at[pl.ds(0, dpn - 1)], r_ar.at[3])
    for c in range(dpn):
        rg_ref[chunk(c)] = fin[c]

    for phase, ref in enumerate((sx, sg)):
        for h in range(2):
            lo = max(1, half * h)
            wait_bytes(ref.at[pl.ds(lo, half * (h + 1) - lo)], s_in.at[2 * phase + h])
    for phase, ref in enumerate((px, pg)):
        for h in range(2):
            lo = max(1, half * h)
            wait_bytes(ref.at[pl.ds(lo, half * (h + 1) - lo)], s_out.at[2 * phase + h])
    for i in range(3):
        far(i).wait_send()
        relay(i).wait_send()

    @pl.when(core != yh)
    def _():
        for i in range(3):
            pair(i).wait_send()

    for copy in links.values():
        copy.wait_send()
    wait_bytes(r1.at[pl.ds(0, dpn - 1)], s_ar.at[0])
    wait_bytes(so.at[pl.ds(0, groups - 1)], s_ar.at[4])
    wait_bytes(ax.at[pl.ds(0, nx - 1)], s_ar.at[1])
    wait_bytes(ay.at[pl.ds(0, yn - 1)], s_ar.at[2])
    wait_bytes(fin.at[pl.ds(0, dpn - 1)], s_ar.at[3])


def on_device(tokens, expert_ids, router_weight, gate_weight, up_weight, down_weight, grad_out):
    sizes = tuple(lax.axis_size(name) for name in ("dp", "tp", "cp"))
    dpn, tpn, cpn = sizes
    groups = tpn * cpn
    t_count, d = tokens.shape
    shard, ff = gate_weight.shape[1:]
    block = pltpu.VMEM((groups, ROWS, 3 * d // 4), BF16)
    wide = 4 * d // dpn
    vmem = pl.BlockSpec(memory_space=pltpu.VMEM)
    dma = pltpu.SemaphoreType.DMA
    nz = dpn // 2
    moe, grad_tokens, router = pl.pallas_call(
        functools.partial(kernel, sizes),
        out_shape=(
            jax.ShapeDtypeStruct((t_count, d), BF16),
            jax.ShapeDtypeStruct((t_count, d), BF16),
            jax.ShapeDtypeStruct((32, d), F32),
        ),
        in_specs=[vmem] * 7,
        out_specs=(vmem,) * 3,
        scratch_shapes=[block] * 8
        + [
            pltpu.VMEM((groups * ROWS, d), BF16),
            pltpu.VMEM((groups * ROWS, d), BF16),
            pltpu.VMEM((groups * ROWS, ff), F32),
            pltpu.VMEM((groups * ROWS, ff), F32),
            pltpu.VMEM((groups * ROWS, ff), F32),
            pltpu.VMEM((groups, 1, LANES), F32),
            pltpu.VMEM((groups, 1, LANES), F32),
            pltpu.VMEM((3, shard, ff), BF16),
            pltpu.VMEM((3, shard, ff), BF16),
            pltpu.VMEM((3, dpn, shard, ff), BF16),
            pltpu.VMEM((32, d), F32),
            pltpu.VMEM((dpn, 8, wide), F32),
            pltpu.VMEM((cpn // 2, 8, wide), F32),
            pltpu.VMEM((2 * tpn, 8, wide), F32),
            pltpu.VMEM((dpn, 8, wide), F32),
            dma((4,)), dma((4,)), dma((4,)), dma((2,)),
            dma((3 * nz,)), dma((3 * nz,)),
            dma((3,)), dma((3,)), dma((3,)), dma((3,)), dma((3,)),
            dma((5,)), dma((5,)),
        ],
        compiler_params=pltpu.CompilerParams(collective_id=0, has_side_effects=True),
        name="experts",
    )(
        tokens, expert_ids.T, router_weight.T, gate_weight, up_weight,
        jnp.swapaxes(down_weight, 1, 2), grad_out,
    )
    return moe, grad_tokens, router[: router_weight.shape[1]].T


def solution(mesh):
    in_specs = (
        P(("dp", "tp", "cp"), None),
        P(("dp", "tp", "cp"), None),
        P(),
        P(("tp", "cp"), "dp", None),
        P(("tp", "cp"), "dp", None),
        P(("tp", "cp"), None, "dp"),
        P(("dp", "tp", "cp"), None),
    )
    out_specs = (P(("dp", "tp", "cp"), None), P(("dp", "tp", "cp"), None), P())
    return jax.shard_map(
        on_device, mesh=mesh, in_specs=in_specs, out_specs=out_specs, check_vma=False
    )
```

```python
import functools

import jax
import jax.numpy as jnp
from jax import lax
from jax.experimental import pallas as pl
from jax.experimental.pallas import tpu as pltpu
from jax.sharding import PartitionSpec as P

MESH = pl.DeviceIdType.MESH
F32 = jnp.float32
BF16 = jnp.bfloat16
ROWS = 16
CAP = 12
LANES = 128


def iota(shape, dim):
    return lax.broadcasted_iota(jnp.int32, shape, dim)


def mm(a, b):
    return lax.dot_general(a, b, (((1,), (0,)), ((), ())), preferred_element_type=F32)


def mm_t(a, b):
    return lax.dot_general(a, b, (((1,), (1,)), ((), ())), preferred_element_type=F32)


def kernel(
    sizes,
    tok_ref, ids_ref, rw_ref, wg_ref, wu_ref, wd_ref, g_ref,
    moe_ref, gt_ref, rg_ref,
    sx, sg, rx, rg, px, pg, cx, cg, xs, gs, act, up, gh, so, si, ws, wr, w, part, r1, ax, ay, fin,
    s_in, r_in, s_out, r_out, s_ring, r_ring, s_far, s_mid, s_pair, r_mid, r_own, s_ar, r_ar,
):
    dpn, tpn, cpn = sizes
    groups = tpn * cpn
    half = groups // 2
    nx = cpn // 2
    nz = dpn // 2
    t_count, d = tok_ref.shape
    q = d // 4
    dp = lax.axis_index("dp")
    tp = lax.axis_index("tp")
    cp = lax.axis_index("cp")
    xi = lax.rem(cp, nx)
    yh = cp // nx
    yn = 2 * tpn
    y = yh * tpn + tp
    z = dp // 2
    core = lax.rem(dp, 2)
    mine = tp * cpn + core * nx + xi

    def shift(dl, h):
        return dl - tpn * ((2 * dl + h) // (tpn + 1))

    xs_up = [lax.rem(xi + dx, nx) for dx in range(nx)]
    xs_down = [lax.rem(xi - dx + nx, nx) for dx in range(nx)]
    cores = [core, 1 - core]

    def column(to_y):
        return lax.rem(to_y, tpn), (to_y // tpn) * nx

    def each_host(h, fn):
        def run(dl, carry):
            to = [column(lax.rem(y + shift(dl, c) + yn, yn)) for c in range(2)]
            first = [
                (core * to[1 - dc][0] + (1 - core) * to[dc][0], core * to[1 - dc][1] + (1 - core) * to[dc][1])
                for dc in range(2)
            ]
            for j in range(2 * nx):
                dx, dc = j // 2, j % 2
                to_tp, base = first[dc]

                def send():
                    expert = to_tp * cpn + cores[dc] * nx + xs_up[dx]
                    fn(dl * (2 * nx) + j, expert, (z * 2 + cores[dc], to_tp, base + xs_up[dx]))

                if j:
                    send()
                else:
                    pl.when(dl > 0)(send)
            return carry

        lax.fori_loop(tpn // 2 * h, tpn // 2 * (h + 1), run, 0)

    def each_home(h, fn):
        def run(dl, carry):
            to_tp, base = column(lax.rem(y - shift(dl, core) + yn, yn))
            for j in range(2 * nx):
                dx, dc = j // 2, j % 2

                def send():
                    fn(dl * (2 * nx) + j, (z * 2 + cores[dc], to_tp, base + xs_down[dx]))

                if j:
                    send()
                else:
                    pl.when(dl > 0)(send)
            return carry

        lax.fori_loop(tpn // 2 * h, tpn // 2 * (h + 1), run, 0)

    def remote(src, dst, send, recv, device):
        return pltpu.make_async_remote_copy(
            src_ref=src, dst_ref=dst, send_sem=send, recv_sem=recv,
            device_id=device, device_id_type=MESH,
        )

    def wait_bytes(ref, sem):
        pltpu.make_async_copy(ref, ref, sem).wait()

    barrier = pltpu.get_barrier_semaphore()

    def greet(to):
        pl.semaphore_signal(barrier, inc=1, device_id=to, device_id_type=MESH)

    def greet_plane(to_tp, carry):
        for to_cp in range(cpn):
            for c in range(2):
                other = (to_tp != tp) | (cp != to_cp) | (core != c)
                pl.when(other)(functools.partial(greet, (z * 2 + c, to_tp, to_cp)))
        return carry

    lax.fori_loop(0, tpn, greet_plane, 0)
    for to in range(dpn):
        pl.when(z != to // 2)(functools.partial(greet, (to, tp, cp)))

    shards = [wg_ref[0], wu_ref[0], wd_ref[0]]
    for i in range(3):
        ws[i] = shards[i]

    @pl.when(core == yh)
    def _():
        for i in range(3):
            w[i, dp] = shards[i]

    tokens = tok_ref[...]
    grads = g_ref[...]
    expert = iota((LANES, t_count), 0)
    hot_t = [(expert == ids_ref[k : k + 1, :]).astype(F32) for k in range(2)]
    both_t = (hot_t[0] + hot_t[1]).astype(BF16)
    upper = (iota((t_count, t_count), 0) < iota((t_count, t_count), 1)).astype(BF16)
    before_t = mm(both_t, upper).astype(BF16)
    span = groups * ROWS
    spread_t = (iota((span, LANES), 0) // ROWS == iota((span, LANES), 1)).astype(BF16)
    slot_t = mm(spread_t, before_t)
    named_t = mm(spread_t, both_t) > 0.5
    row_t = lax.rem(iota((span, t_count), 0), ROWS)

    def choice(named, slot, row, j):
        wanted = row if j is None else jnp.where(row >= CAP, 3 * (row - CAP) + j, -1)
        return (named & (slot == wanted.astype(F32))).astype(BF16)

    main_t = choice(named_t, slot_t, row_t, None)
    tail_t = [choice(named_t, slot_t, row_t, j) for j in range(3)]

    def pack_home(values, out):
        for j in range(3):
            piece = mm(main_t, values[:, q * j : q * (j + 1)]) + mm(tail_t[j], values[:, 3 * q :])
            out[:, :, q * j : q * (j + 1)] = piece.astype(BF16).reshape(groups, ROWS, q)

    pack_home(tokens, sx)

    pl.semaphore_wait(barrier, 2 * groups - 1 + dpn - 2)

    hop = (yn // 4) * (1 - 2 * core)
    hop_tp, hop_base = column(lax.rem(y + hop + yn, yn))
    from_yh = lax.rem(y - hop + yn, yn) // tpn

    def far(i):
        return remote(
            ws.at[i], wr.at[i], s_far.at[i], r_mid.at[i], (dp, hop_tp, hop_base + xi)
        )

    def relay(i):
        return remote(
            wr.at[i], w.at[i, dp], s_mid.at[i], r_own.at[i],
            (z * 2 + from_yh, hop_tp, hop_base + xi),
        )

    def pair(i):
        return remote(
            ws.at[i], w.at[i, dp], s_pair.at[i], r_own.at[i], (z * 2 + 1 - core, tp, cp)
        )

    for i in range(3):
        far(i).start()

    @pl.when(core != yh)
    def _():
        for i in range(3):
            pair(i).start()

    steps = nz // 2

    def ring(sign, step, i):
        at = pl.ds(lax.rem(z - sign * step + nz, nz) * 2, 2)
        index = ((0 if sign > 0 else steps) + step) * 3 + i
        return remote(
            w.at[i, at], w.at[i, at], s_ring.at[index], r_ring.at[index],
            (lax.rem(z + sign + nz, nz) * 2 + core, tp, cp),
        )

    links = {}
    for sign in (1, -1):
        for s in range(steps):
            for i in range(3):
                if s + 1 < steps or (i == 1) == (sign < 0):
                    links[sign, s, i] = ring(sign, s, i)

    def enter_ring():
        for i in range(3):
            for sign in (1, -1):
                if (sign, 0, i) in links:
                    links[sign, 0, i].start()

    def ring_step(s, chunks=(0, 1, 2)):
        for i in chunks:
            for sign in (1, -1):
                if (sign, s, i) in links:
                    links[sign, s, i].wait_recv()
                if (sign, s + 1, i) in links:
                    links[sign, s + 1, i].start()

    def send_in(src, dst, phase):
        for h in range(2):
            index = 2 * phase + h
            each_host(h, lambda r, expert, to: remote(
                src.at[expert], dst.at[r], s_in.at[index], r_in.at[index], to
            ).start())

    @pl.when(core == yh)
    def _():
        for i in range(3):
            wait_bytes(w.at[i, pl.ds(0, 1)], r_own.at[i])
        enter_ring()

    for i in range(3):
        far(i).wait_recv()
        relay(i).start()
    send_in(sx, rx, 0)

    @pl.when(core != yh)
    def _():
        for i in range(3):
            wait_bytes(w.at[i, pl.ds(0, 2)], r_own.at[i])
        enter_ring()

    pack_home(grads, sg)
    send_in(sg, rg, 1)
    rx[0] = sx[mine]
    rg[0] = sg[mine]

    logits = mm_t(tokens, rw_ref[...])
    ecount = rw_ref.shape[0]
    hot = [hot_t[k].T for k in range(2)]
    both = hot[0] + hot[1]
    chosen = [jnp.sum(logits * hot[k][:, :ecount], axis=1, keepdims=True) for k in range(2)]
    mixing = [
        1.0 / (1.0 + jnp.exp(chosen[1] - chosen[0])),
        1.0 / (1.0 + jnp.exp(chosen[0] - chosen[1])),
    ]
    if steps > 1:
        ring_step(0)
    lower = (iota((t_count, t_count), 1) < iota((t_count, t_count), 0)).astype(BF16)
    before = mm(lower, both.astype(BF16)).astype(BF16)
    spread = (iota((LANES, span), 1) // ROWS == iota((LANES, span), 0)).astype(BF16)
    slot = mm(before, spread)
    row = lax.rem(iota((t_count, span), 1), ROWS)
    slots = [jnp.sum(before.astype(F32) * hot[k], axis=1, keepdims=True) for k in range(2)]
    picks = []
    for k in range(2):
        named = mm(hot[k].astype(BF16), spread) > 0.5
        picks.append([choice(named, slot, row, None)] + [choice(named, slot, row, j) for j in range(3)])
    for s in range(1, steps - 1):
        ring_step(s)

    size = half * ROWS
    pr, qr = iota((size, size), 0), iota((size, size), 1)
    same = pr // ROWS == qr // ROWS
    pr, qr = lax.rem(pr, ROWS), lax.rem(qr, ROWS)
    unpack = [
        (same & (pr < CAP) & (qr >= CAP) & (pr == 3 * (qr - CAP) + j)).astype(BF16) for j in range(3)
    ]
    repack = [
        (same & (qr < CAP) & (pr >= CAP) & (qr == 3 * (pr - CAP) + j)).astype(BF16) for j in range(3)
    ]
    is_main = lax.rem(iota((size, q), 0), ROWS) < CAP

    def open_rows(ref, h):
        packed = ref[half * h : half * (h + 1)].reshape(size, 3 * q)
        tail = sum(mm(unpack[j], packed[:, q * j : q * (j + 1)]) for j in range(3))
        return jnp.concatenate([packed, tail.astype(BF16)], axis=1)

    def close_rows(values, ref, h):
        for j in range(3):
            piece = jnp.where(
                is_main, values[:, q * j : q * (j + 1)].astype(F32), mm(repack[j], values[:, 3 * q :])
            )
            ref[half * h : half * (h + 1), :, q * j : q * (j + 1)] = piece.astype(BF16).reshape(
                half, ROWS, q
            )

    def weight(i):
        return w[i].reshape(d, w.shape[3])

    def wait_in(ref, phase, h):
        lo = max(1, half * h)
        wait_bytes(ref.at[pl.ds(lo, half * (h + 1) - lo)], r_in.at[2 * phase + h])

    def send_out(src, dst, phase, h):
        index = 2 * phase + h
        each_home(h, lambda r, to: remote(
            src.at[r], dst.at[mine], s_out.at[index], r_out.at[phase], to
        ).start())

    for h in range(2):
        wait_in(rx, 0, h)
        xs[size * h : size * (h + 1)] = open_rows(rx, h)
    for h in range(2):
        wait_in(rg, 1, h)
        gs[size * h : size * (h + 1)] = open_rows(rg, h)
    ring_step(steps - 1, (0, 1))
    for h in range(2):
        at = slice(size * h, size * (h + 1))
        act[at] = mm(xs[at], weight(0))
        up[at] = mm(xs[at], weight(1))
    ring_step(steps - 1, (2,))
    hiddens = []
    lanes = iota((size, LANES), 1)
    own_lane = lanes == lax.rem(iota((size, LANES), 0), ROWS)
    for h in range(2):
        at = slice(size * h, size * (h + 1))
        gate = act[at]
        hidden = (gate * jax.nn.sigmoid(gate) * up[at]).astype(BF16)
        hiddens.append(hidden)
        grad_hidden = mm(gs[at], weight(2))
        gh[at] = grad_hidden
        score = jnp.sum(hidden.astype(F32) * grad_hidden, axis=1, keepdims=True)
        table = jnp.where(own_lane, score, 0.0).reshape(half, ROWS, LANES)
        so[half * h : half * (h + 1)] = jnp.sum(table, axis=1, keepdims=True)
    for h in range(2):
        each_home(h, lambda r, to: remote(so.at[r], si.at[mine], s_ar.at[4], r_ar.at[4], to).start())
    si[mine] = so[0]
    for h in range(2):
        close_rows(mm_t(hiddens[h], weight(2)).astype(BF16), px, h)
        send_out(px, cx, 0, h)
    cx[mine] = px[0]
    for h in range(2):
        at = slice(size * h, size * (h + 1))
        grad_hidden, gate, upper_act = gh[at], act[at], up[at]
        sigma = jax.nn.sigmoid(gate)
        grad_gate = (grad_hidden * upper_act * sigma * (1.0 + gate * (1.0 - sigma))).astype(BF16)
        grad_up = (grad_hidden * gate * sigma).astype(BF16)
        back = mm_t(grad_gate, weight(0)) + mm_t(grad_up, weight(1))
        close_rows(back.astype(BF16), pg, h)
    cg[mine] = pg[0]

    def home_rows(ref, k):
        packed = ref[...].reshape(span, 3 * q)
        main = mm(picks[k][0], packed)
        tail = sum(mm(picks[k][1 + j], packed[:, q * j : q * (j + 1)]) for j in range(3))
        return jnp.concatenate([main, tail], axis=1)

    wait_bytes(si.at[pl.ds(0, groups - 1)], r_ar.at[4])
    rest = si[...].reshape(groups, LANES)
    pieces = []
    for _ in range(3):
        pieces.append(rest.astype(BF16))
        rest = rest - pieces[-1].astype(F32)
    token_lane = iota((t_count, LANES), 1).astype(F32)
    scores = []
    for k in range(2):
        of_expert = hot[k][:, :groups].astype(BF16)
        found = sum(mm(of_expert, piece) for piece in pieces)
        scores.append(
            jnp.sum(jnp.where(token_lane == slots[k], found, 0.0), axis=1, keepdims=True)
        )
    mean = mixing[0] * scores[0] + mixing[1] * scores[1]
    dense = sum(hot[k] * (mixing[k] * (scores[k] - mean)) for k in range(2))
    dense_t = dense.T.astype(BF16)
    part[...] = mm(dense_t, tokens)[: part.shape[0]]

    cw = r1.shape[2]
    nb = d // cw

    def chunk(c):
        return slice(8 * (c // nb), 8 * (c // nb) + 8), slice(cw * (c % nb), cw * (c % nb + 1))

    for to in range(dpn):
        rows_to, cols_to = chunk(to)

        @pl.when(dp != to)
        def _():
            remote(
                part.at[rows_to, cols_to], r1.at[dp], s_ar.at[0], r_ar.at[0], (to, tp, cp)
            ).start()

        @pl.when(dp == to)
        def _():
            r1[dp] = part[rows_to, cols_to]

    router_back = mm(dense.astype(BF16)[:, :ecount], rw_ref[...])

    wait_bytes(r1.at[pl.ds(0, dpn - 1)], r_ar.at[0])
    ax[xi] = jnp.sum(r1[...], axis=0)
    for o in range(1, nx):
        remote(
            ax.at[xi], ax.at[xi], s_ar.at[1], r_ar.at[1], (dp, tp, yh * nx + xs_up[o])
        ).start()
    send_out(pg, cg, 1, 0)
    wait_bytes(ax.at[pl.ds(0, nx - 1)], r_ar.at[1])
    ay[y] = jnp.sum(ax[...], axis=0)
    for o in range(1, yn):
        to_tp, base = column(lax.rem(y + o, yn))
        remote(ay.at[y], ay.at[y], s_ar.at[2], r_ar.at[2], (dp, to_tp, base + xi)).start()
    send_out(pg, cg, 1, 1)

    wait_bytes(cx.at[pl.ds(0, groups - 1)], r_out.at[0])
    moe_ref[...] = (mixing[0] * home_rows(cx, 0) + mixing[1] * home_rows(cx, 1)).astype(BF16)

    wait_bytes(ay.at[pl.ds(0, yn - 1)], r_ar.at[2])
    fin[dp] = jnp.sum(ay[...], axis=0)
    for to in range(dpn):
        @pl.when(dp != to)
        def _():
            remote(fin.at[dp], fin.at[dp], s_ar.at[3], r_ar.at[3], (to, tp, cp)).start()

    wait_bytes(cg.at[pl.ds(0, groups - 1)], r_out.at[1])
    gt_ref[...] = (
        mixing[0] * home_rows(cg, 0) + mixing[1] * home_rows(cg, 1) + router_back
    ).astype(BF16)

    wait_bytes(fin.at[pl.ds(0, dpn - 1)], r_ar.at[3])
    for c in range(dpn):
        rg_ref[chunk(c)] = fin[c]

    for phase, ref in enumerate((sx, sg)):
        for h in range(2):
            lo = max(1, half * h)
            wait_bytes(ref.at[pl.ds(lo, half * (h + 1) - lo)], s_in.at[2 * phase + h])
    for phase, ref in enumerate((px, pg)):
        for h in range(2):
            lo = max(1, half * h)
            wait_bytes(ref.at[pl.ds(lo, half * (h + 1) - lo)], s_out.at[2 * phase + h])
    for i in range(3):
        far(i).wait_send()
        relay(i).wait_send()

    @pl.when(core != yh)
    def _():
        for i in range(3):
            pair(i).wait_send()

    for copy in links.values():
        copy.wait_send()
    wait_bytes(r1.at[pl.ds(0, dpn - 1)], s_ar.at[0])
    wait_bytes(so.at[pl.ds(0, groups - 1)], s_ar.at[4])
    wait_bytes(ax.at[pl.ds(0, nx - 1)], s_ar.at[1])
    wait_bytes(ay.at[pl.ds(0, yn - 1)], s_ar.at[2])
    wait_bytes(fin.at[pl.ds(0, dpn - 1)], s_ar.at[3])


def on_device(tokens, expert_ids, router_weight, gate_weight, up_weight, down_weight, grad_out):
    sizes = tuple(lax.axis_size(name) for name in ("dp", "tp", "cp"))
    dpn, tpn, cpn = sizes
    groups = tpn * cpn
    t_count, d = tokens.shape
    shard, ff = gate_weight.shape[1:]
    block = pltpu.VMEM((groups, ROWS, 3 * d // 4), BF16)
    wide = 4 * d // dpn
    vmem = pl.BlockSpec(memory_space=pltpu.VMEM)
    dma = pltpu.SemaphoreType.DMA
    nz = dpn // 2
    moe, grad_tokens, router = pl.pallas_call(
        functools.partial(kernel, sizes),
        out_shape=(
            jax.ShapeDtypeStruct((t_count, d), BF16),
            jax.ShapeDtypeStruct((t_count, d), BF16),
            jax.ShapeDtypeStruct((32, d), F32),
        ),
        in_specs=[vmem] * 7,
        out_specs=(vmem,) * 3,
        scratch_shapes=[block] * 8
        + [
            pltpu.VMEM((groups * ROWS, d), BF16),
            pltpu.VMEM((groups * ROWS, d), BF16),
            pltpu.VMEM((groups * ROWS, ff), F32),
            pltpu.VMEM((groups * ROWS, ff), F32),
            pltpu.VMEM((groups * ROWS, ff), F32),
            pltpu.VMEM((groups, 1, LANES), F32),
            pltpu.VMEM((groups, 1, LANES), F32),
            pltpu.VMEM((3, shard, ff), BF16),
            pltpu.VMEM((3, shard, ff), BF16),
            pltpu.VMEM((3, dpn, shard, ff), BF16),
            pltpu.VMEM((32, d), F32),
            pltpu.VMEM((dpn, 8, wide), F32),
            pltpu.VMEM((cpn // 2, 8, wide), F32),
            pltpu.VMEM((2 * tpn, 8, wide), F32),
            pltpu.VMEM((dpn, 8, wide), F32),
            dma((4,)), dma((4,)), dma((4,)), dma((2,)),
            dma((3 * nz,)), dma((3 * nz,)),
            dma((3,)), dma((3,)), dma((3,)), dma((3,)), dma((3,)),
            dma((5,)), dma((5,)),
        ],
        compiler_params=pltpu.CompilerParams(collective_id=0, has_side_effects=True),
        name="experts",
    )(
        tokens, expert_ids.T, router_weight.T, gate_weight, up_weight,
        jnp.swapaxes(down_weight, 1, 2), grad_out,
    )
    return moe, grad_tokens, router[: router_weight.shape[1]].T


def solution(mesh):
    in_specs = (
        P(("dp", "tp", "cp"), None),
        P(("dp", "tp", "cp"), None),
        P(),
        P(("tp", "cp"), "dp", None),
        P(("tp", "cp"), "dp", None),
        P(("tp", "cp"), None, "dp"),
        P(("dp", "tp", "cp"), None),
    )
    out_specs = (P(("dp", "tp", "cp"), None), P(("dp", "tp", "cp"), None), P())
    return jax.shard_map(
        on_device, mesh=mesh, in_specs=in_specs, out_specs=out_specs, check_vma=False
    )
```
